256 devices in a mesh: tile: 64 (over x, z_hi, y, core), lev: 4 (over z_lo).
Axes of the slice: x: 4, y: 4, z: 8 (z_hi: 2, z_lo: 4; z = z_hi * 4 + z_lo), core: 2. Of those that a mesh axis runs over, the one named last changes fastest.
Arguments:
- control: float32 [80, 32, 16384], P(None, 'lev', 'tile'), may hold values from -6 to 6
- ensemble: bfloat16 [80, 32, 16384], P(None, 'lev', 'tile'), may hold values from -6 to 6
- loc_blocks: bfloat16 [128, 9, 128, 128], P('tile'), may hold values from -0.1875 to 0.1875
- neighbours: int32 [128, 9], P('tile'), may hold values from 0 to 127, as said below
- vert_band: float32 [32, 9], replicated, may hold values from 0.1 to 0.6
- channel_weights: float32 [16, 32], P(None, 'lev'), may hold values from -1 to 1
- innovation: float32 [16, 16384], P(None, 'tile'), may hold values from -6 to 6
- inv_error: float32 [16, 16384], P(None, 'tile'), may hold values from 0.25 to 4
Outputs:
- grad_first: float32 [80, 32, 16384], P(None, 'lev', 'tile')
- grad_second: float32 [80, 32, 16384], P(None, 'lev', 'tile')
- costs: float32 [2], replicated
The draws below stay inside these ranges and needn't reach their ends.
Inputs may be any that keep to these rules, and one draw needn't show every extreme that they name: neighbours[b,0] = b; neighbours[b,1] lies in tile b // 2 - 1 and neighbours[b,2] in tile b // 2 + 1, tiles counted cyclically modulo 64; every other entry lies in one of these three tiles; block n belongs to tile n // 2.
All inputs are finite; a program needn't handle non-finite values.
Results may differ from the reference program's by a relative error of at most 0.005.
Values may be sent and summed in bfloat16 or wider, within the bound.
No kernel may reach another device: no remote copies, remote signals or barrier semaphores. Data moves between devices by JAX's collectives and lax.ppermute only.
A program may use at most 64 MiB of HBM per device.

```python
import math
import jax
import jax.numpy as jnp
from jax import lax

M = 80
BPD = 2
NBR = 9
HV = 4
K = 16
LEV = 32
NBLK = 128
PT = 16384


def draw_neighbours(key, part):
    tiles = NBLK // BPD
    blocks = jnp.arange(NBLK, dtype=jnp.int32)
    tile_of = blocks // BPD
    key_off, key_blk = jax.random.split(jax.random.fold_in(key, 17))
    offsets = jax.random.randint(key_off, (NBLK, NBR), -1, 2).astype(jnp.int32)
    column = jnp.arange(NBR, dtype=jnp.int32)[None, :]
    offsets = jnp.where(column == 1, -1, jnp.where(column == 2, 1, offsets))
    inner = jax.random.randint(key_blk, (NBLK, NBR), 0, BPD).astype(jnp.int32)
    chosen = jnp.mod(tile_of[:, None] + offsets, tiles) * BPD + inner
    chosen = jnp.where(column == 0, blocks[:, None], chosen)
    return chosen.astype(jnp.int32)


def block_levels(rng, shape, cuts, least, largest):
    def one(axis_at, parts):
        steps = jax.random.uniform(jax.random.fold_in(jax.random.fold_in(rng, 6), axis_at), (parts,), jnp.float32, least / len(cuts), largest / len(cuts))
        return jnp.repeat(jnp.exp(steps), shape[axis_at] // parts).reshape((-1,) + (1,) * (len(shape) - axis_at - 1))

    factor_of = one(*cuts[0])
    for cut in cuts[1:]:
        factor_of = factor_of * one(*cut)
    return factor_of


def centred(own_key, dims, scale, most, shards=(), kind=jnp.bfloat16):
    drawn = jax.random.normal(own_key, dims, jnp.float32) * scale
    if len(shards) > 0:
        drawn = block_levels(own_key, dims, shards, -0.22, 0.18) * drawn
    return jnp.clip(drawn, min=-most, max=most).astype(kind)


def setup_inputs(seed: int = 0) -> dict:
    streams_of = jax.random.split(jax.random.key(seed), 9)
    return {
        "control": centred(streams_of[0], (M, LEV, PT), 1.0, 6.0, ((1, 4), (2, 64)), jnp.float32),
        "ensemble": centred(streams_of[1], (M, LEV, PT), 1.0, 6.0, ((1, 4), (2, 64))),
        "loc_blocks": centred(streams_of[2], (NBLK, NBR, 128, 128), (128 * NBR) ** -0.5, 0.1875, ((0, 64),)),
        "neighbours": draw_neighbours(jax.random.fold_in(streams_of[8], 71), 0),
        "vert_band": jnp.clip(jax.random.uniform(streams_of[4], (LEV, 2 * HV + 1), jnp.float32, 0.1, 0.6), 0.1, 0.6),
        "channel_weights": centred(streams_of[5], (K, LEV), LEV ** -0.5, 1.0, ((1, 4),), jnp.float32),
        "innovation": centred(streams_of[6], (K, PT), 1.0, 6.0, ((1, 64),), jnp.float32),
        "inv_error": jnp.clip(jnp.exp(math.log(4.0) - 2.7725887 * jax.random.uniform(streams_of[7], (K, PT), jnp.float32) ** block_levels(streams_of[7], (K, PT), ((1, 64),), -0.2, 0.2)), 0.25, 4.0),
    }


def vertical(field, vert_band):
    padded = jnp.pad(field, ((0, 0), (HV, HV), (0, 0)))
    total = jnp.zeros_like(field)
    for s in range(2 * HV + 1):
        total = total + vert_band[:, s][None, :, None] * padded[:, s:s + LEV, :]
    return total

def vertical_adjoint(field, vert_band):
    total = jnp.zeros_like(field)
    for s in range(2 * HV + 1):
        weighted = vert_band[:, s][None, :, None] * field
        padded = jnp.pad(weighted, ((0, 0), (HV, HV), (0, 0)))
        total = total + padded[:, 2 * HV - s:2 * HV - s + LEV, :]
    return total

def evaluate(control, ensemble, blocks_f, neighbours, vert_band, channel_weights, innovation, inv_error):
    norm_factor = 1.0 / math.sqrt(M - 1)
    avb = vertical(control, vert_band).astype(jnp.bfloat16)

    def forward(member):
        pieces = member.astype(jnp.float32).reshape(LEV, NBLK, 128)[:, neighbours, :]
        out = jnp.einsum('lbjc,bjic->lbi', pieces, blocks_f)
        return out.reshape(LEV, PT)
    u = lax.map(forward, avb)
    dx = lax.optimization_barrier(jnp.sum(ensemble.astype(jnp.float32) * u, axis=0)) * norm_factor
    hx = jnp.einsum('kl,lp->kp', channel_weights, dx, precision=lax.Precision.HIGHEST)
    diff = hx - innovation
    q = inv_error * diff
    cost = (0.5 * jnp.sum(control * control) + 0.5 * jnp.sum(q * diff)) / (M * LEV * PT)
    dxa = jnp.einsum('kl,kp->lp', channel_weights, q, precision=lax.Precision.HIGHEST)
    ua = (ensemble.astype(jnp.float32) * dxa[None] * norm_factor).astype(jnp.bfloat16)

    def backward(member):
        terms = jnp.einsum('lbi,bjic->lbjc', member.astype(jnp.float32).reshape(LEV, NBLK, 128), blocks_f)
        spread = jnp.zeros((LEV, NBLK, 128), jnp.float32).at[:, neighbours.reshape(-1), :].add(terms.reshape(LEV, NBLK * NBR, 128))
        return spread.reshape(LEV, PT)
    ava = lax.map(backward, ua)
    grad = control + vertical_adjoint(ava, vert_band)
    return (grad, cost)

def reference(control, ensemble, loc_blocks, neighbours, vert_band, channel_weights, innovation, inv_error):
    blocks_f = loc_blocks.astype(jnp.float32)
    grad_first, cost0 = evaluate(control, ensemble, blocks_f, neighbours, vert_band, channel_weights, innovation, inv_error)
    tau = 0.5 / jnp.sqrt(jnp.mean(grad_first * grad_first) + 1e-06)
    second = control - tau * grad_first
    grad_second, cost1 = evaluate(second, ensemble, blocks_f, neighbours, vert_band, channel_weights, innovation, inv_error)
    return (grad_first, grad_second, jnp.stack([cost0, cost1]))
```

```python
import math

import jax
import jax.numpy as jnp
from jax import lax
from jax.experimental import pallas as pl
from jax.experimental.pallas import tpu as pltpu
from jax.sharding import PartitionSpec as P

HV = 4
NS = 2 * HV + 1
STEP = 0.5
F32 = jnp.float32
BF16 = jnp.bfloat16
VM = pl.BlockSpec(memory_space=pltpu.VMEM)
SM = pl.BlockSpec(memory_space=pltpu.SMEM)


def call(body, outs, args, scalars, scratch=(), flops=0):
    specs = [SM] * scalars + [VM] * (len(args) - scalars)
    moved = sum(a.size * a.dtype.itemsize for a in args)
    moved += sum(math.prod(o.shape) * jnp.dtype(o.dtype).itemsize for o in outs)
    return pl.pallas_call(
        body,
        out_shape=tuple(outs),
        in_specs=specs,
        out_specs=tuple(VM for _ in outs),
        scratch_shapes=list(scratch),
        cost_estimate=pl.CostEstimate(flops=flops, bytes_accessed=moved, transcendentals=0),
        compiler_params=pltpu.CompilerParams(vmem_limit_bytes=48 * 1024 * 1024),
    )(*args)


def sds(shape, dtype):
    return jax.ShapeDtypeStruct(shape, dtype)


def split3(x):
    hi = x.astype(BF16)
    rest = x - hi.astype(F32)
    mid = rest.astype(BF16)
    lo = (rest - mid.astype(F32)).astype(BF16)
    return hi, mid, lo


def join3(hi, mid, lo):
    return (hi.astype(F32) + mid.astype(F32)) + lo.astype(F32)


def pack_ens_kernel(scal, ens, *outs):
    share = outs[0].shape[0]
    for k in range(4):
        outs[k][...] = ens[pl.ds(share * (scal[2] ^ k), share)]


def pack_ctl_kernel(scal, ctl, wt, *outs):
    share = outs[0].shape[0] - 3
    parts = split3(wt[...])
    for k in range(4):
        outs[k][pl.ds(0, share)] = ctl[pl.ds(share * (scal[2] ^ k), share)].astype(BF16)
        for i in range(3):
            outs[k][share + i] = parts[i]
    sq = jnp.zeros(outs[4].shape, F32)

    def body(m, acc):
        v = ctl[m]
        return acc + v * v

    outs[4][...] = lax.fori_loop(0, ctl.shape[0], body, sq, unroll=4)


def densify_kernel(scal, nb, loc, inv, inn, vb, d_own, x_core, x_edge, vw, vwt, acc):
    tile = scal[0]
    core_rel = 2 - 2 * (tile & 1)
    acc[...] = jnp.zeros(acc.shape, F32)
    for b in range(2):
        for j in range(loc.shape[1]):
            n = nb[b, j]
            rel = ((n >> 1) - tile + 65) & 63
            role = jnp.where(rel == 1, 0, jnp.where(rel == core_rel, 1, 2))
            slot = b * 6 + role * 2 + (n & 1)
            acc[slot] = acc[slot] + loc[b, j].astype(F32)
    for role, out in enumerate((d_own, x_core, x_edge)):
        for b in range(2):
            for h in range(2):
                out[128 * b : 128 * b + 128, 128 * h : 128 * h + 128] = acc[
                    b * 6 + role * 2 + h
                ].astype(BF16)
    for out in (x_core, x_edge):
        for i, v in enumerate(split3(inv[...]) + split3(inn[...])):
            out[256 + 16 * i : 272 + 16 * i, :] = v
    lev = vb.shape[0]
    row = lax.broadcasted_iota(jnp.int32, (lev, 128), 0)
    for s in range(NS):
        col = jnp.broadcast_to(vb[:, s : s + 1], (lev, 128))
        src = row + (s - HV)
        vw[s] = jnp.where((src >= 0) & (src < lev), col, 0.0)
        src = row + (HV - s)
        moved = pltpu.roll(col, (s - HV) % lev, 0)
        vwt[s] = jnp.where((src >= 0) & (src < lev), moved, 0.0)


def assemble_kernel(scal, e0, e1, e2, e3, out):
    for k, e in enumerate((e0, e1, e2, e3)):
        out[:, scal[1] ^ k] = e[...]


def forward_part(src, vw, avb, umat, ens3, dmats, w, hxs, norm):
    ms = src.shape[0]
    lev = 32

    def smooth(m, _):
        block = src[m].reshape(lev, 256)
        cols = []
        for h in range(2):
            a = block[:, 128 * h : 128 * h + 128]
            tot = vw[HV] * a
            for s in range(NS):
                if s != HV:
                    tot = tot + vw[s] * pltpu.roll(a, (HV - s) % lev, 0)
            cols.append(tot)
        avb[pl.ds(pl.multiple_of(lev * m, lev), lev), :] = jnp.concatenate(cols, axis=1).astype(
            BF16
        )
        return 0

    lax.fori_loop(0, ms, smooth, 0)
    for ens, d, hx in zip(ens3, dmats, hxs):
        umat[...] = lax.dot_general(
            avb[...], d, (((1,), (1,)), ((), ())), preferred_element_type=F32
        )

        def member(m, acc):
            e = ens[m].astype(F32).reshape(lev, 256)
            return acc + e * umat[pl.ds(pl.multiple_of(lev * m, lev), lev), :]

        dx = lax.fori_loop(0, ms, member, jnp.zeros((lev, 256), F32), unroll=2)
        hx(
            jnp.dot(
                w[:, 0:lev], dx * norm, precision=lax.Precision.HIGHEST, preferred_element_type=F32
            )
        )


def adjoint_part(qs, wt, vwt, ens3, dmats, ua, umat, out, norm):
    ms = out.shape[0]
    lev = 32
    for r, (q, ens, d) in enumerate(zip(qs, ens3, dmats)):
        dxa = (
            jnp.dot(
                wt[:, 0:16], q, precision=lax.Precision.HIGHEST, preferred_element_type=F32
            )
            * norm
        )

        def member(m, _):
            e = ens[m].astype(F32).reshape(lev, 256)
            ua[pl.ds(pl.multiple_of(lev * m, lev), lev), :] = (e * dxa).astype(BF16)
            return 0

        lax.fori_loop(0, ms, member, 0, unroll=2)
        part = jnp.dot(ua[...], d, preferred_element_type=F32)
        if r == 0:
            umat[...] = part
        else:
            umat[...] = umat[...] + part

    def spread(m, _):
        block = umat[pl.ds(pl.multiple_of(lev * m, lev), lev), :]
        cols = []
        for h in range(2):
            a = block[:, 128 * h : 128 * h + 128]
            tot = vwt[HV] * a
            for s in range(NS):
                if s != HV:
                    tot = tot + vwt[s] * pltpu.roll(a, (s - HV) % lev, 0)
            cols.append(tot)
        out[m] = jnp.concatenate(cols, axis=1).reshape(4, 8, 256)
        return 0

    lax.fori_loop(0, ms, spread, 0)


def dmats_of(d_own, x_core, x_edge):
    return d_own[...], x_core[0:256, :], x_edge[0:256, :]


def obs_of(x):
    return (
        join3(x[256:272, :], x[272:288, :], x[288:304, :]),
        join3(x[304:320, :], x[320:336, :], x[336:352, :]),
    )


def first_kernel(
    norm, scal, c0, c1, c2, c3, e_own, e_core, e_edge, d_own, x_core, x_edge, vw,
    cm, hx_core, hx_oe, w, wt, src, wsq, avb, umat,
):
    share = src.shape[0]
    wsq[...] = jnp.zeros(wsq.shape, F32)
    for k, c in enumerate((c0, c1, c2, c3)):
        group = scal[1] ^ k
        val = c[pl.ds(0, share)]
        cm[:, group] = val
        src[:, group] = val.astype(F32)
        wsq[pl.ds(pl.multiple_of(8 * group, 8), 8), :] = join3(
            c[share], c[share + 1], c[share + 2]
        )[:, 0:128]
    w[...] = wsq[...].T[0:16, :]
    wt[...] = wsq[0:32, :]

    def put_own(v):
        hx_oe[0:16, :] = v

    def put_core(v):
        hx_core[...] = v

    def put_edge(v):
        hx_oe[16:32, :] = v

    forward_part(
        src, vw, avb, umat, (e_own, e_core, e_edge), dmats_of(d_own, x_core, x_edge), w,
        (put_own, put_core, put_edge), norm,
    )


def second_kernel(
    norm, scal, h_oe, h_core, inv, inn, cm, e_own, e_core, e_edge, d_own, x_core, x_edge,
    vw, vwt, w, wt, s0, a0, a1, a2, a3, hx_core, hx_oe, adj, ua, umat,
):
    share = adj.shape[0]
    ic, yc = obs_of(x_core)
    ie, ye = obs_of(x_edge)
    qs = (
        inv[...] * (h_oe[0:16, :] - inn[...]),
        ic * (h_core[...] - yc),
        ie * (h_oe[16:32, :] - ye),
    )
    ens3 = (e_own, e_core, e_edge)
    dmats = dmats_of(d_own, x_core, x_edge)
    adjoint_part(qs, wt, vwt, ens3, dmats, ua, umat, adj, norm)
    for k, a in enumerate((a0, a1, a2, a3)):
        a[...] = adj[:, scal[1] ^ k].astype(BF16)

    def total(m, carry):
        gg, cg = carry
        c = cm[m].astype(F32)
        g = c + adj[m]
        adj[m] = g
        return gg + jnp.sum(g * g, axis=0), cg + jnp.sum(c * g, axis=0)

    zero = jnp.zeros((8, 256), F32)
    gg, cg = lax.fori_loop(0, share, total, (zero, zero))

    def put_own(v):
        hx_oe[0:16, :] = v

    def put_core(v):
        hx_core[0:16, :] = v

    def put_edge(v):
        hx_oe[16:32, :] = v

    forward_part(
        adj, vw, ua, umat, ens3, dmats, w, (put_own, put_core, put_edge), norm
    )
    hx_core[16:24, :] = jnp.zeros((8, 256), F32)
    hx_core[16:17, :] = jnp.sum(s0[...], axis=0, keepdims=True)
    hx_core[17:18, :] = jnp.sum(gg, axis=0, keepdims=True)
    hx_core[18:19, :] = jnp.sum(cg, axis=0, keepdims=True)


def sums_kernel(hs, h_core, h1_oe, h1_core, inv, inn, x_core, out):
    ic, yc = obs_of(x_core)

    def rows(h1, i, y, d):
        diff = h1 - y
        q = i * diff
        return [
            jnp.sum(q * diff, axis=0, keepdims=True),
            jnp.sum(q * d, axis=0, keepdims=True),
            jnp.sum(i * d * d, axis=0, keepdims=True),
        ]

    own = rows(h1_oe[0:16, :], inv[...], inn[...], hs[0:16, :])
    core = rows(h1_core[...], ic, yc, h_core[...])
    out[...] = hs[32:40, :]
    for i in range(3):
        out[3 + i : 4 + i, :] = own[i] + core[i]


def third_kernel(
    norm, scal, h_oe, h_core, inv, e_own, e_core, e_edge, d_own, x_core, x_edge,
    vwt, wt, a0, a1, a2, a3, adj, ua, umat,
):
    ic, _ = obs_of(x_core)
    ie, _ = obs_of(x_edge)
    qs = (inv[...] * h_oe[0:16, :], ic * h_core[...], ie * h_oe[16:32, :])
    adjoint_part(
        qs, wt, vwt, (e_own, e_core, e_edge), dmats_of(d_own, x_core, x_edge), ua, umat, adj,
        norm,
    )
    for k, a in enumerate((a0, a1, a2, a3)):
        a[...] = adj[:, scal[1] ^ k].astype(BF16)


def grad_first_kernel(scal, ctl, a0, a1, a2, a3, out):
    share = a0.shape[0]
    for k, a in enumerate((a0, a1, a2, a3)):
        at = pl.ds(share * (scal[2] ^ k), share)
        out[at] = ctl[at] + a[...].astype(F32)


def grad_second_kernel(count, scal, g1, a0, a1, a2, a3, sums, out, costs):
    tot = jnp.sum(sums[...], axis=1, keepdims=True)
    cc, gg, cg = tot[0:1], tot[1:2], tot[2:3]
    dd, qd, rd = tot[3:4], tot[4:5], tot[5:6]
    tau = STEP / jnp.sqrt(gg / count + 1e-06)
    first = 0.5 * cc + 0.5 * dd
    second = 0.5 * (cc - 2.0 * tau * cg + tau * tau * gg) + 0.5 * (
        dd - 2.0 * tau * qd + tau * tau * rd
    )
    costs[0:1, :] = jnp.broadcast_to(first / count, (1, 128))
    costs[1:2, :] = jnp.broadcast_to(second / count, (1, 128))
    costs[2:8, :] = jnp.zeros((6, 128), F32)
    tb = jnp.broadcast_to(tau, (8, 256))
    share = a0.shape[0]
    for k, a in enumerate((a0, a1, a2, a3)):

        def body(m, _, a=a, k=k):
            at = share * (scal[2] ^ k) + m
            g = g1[at]
            out[at] = g - tb * (g + a[m].astype(F32))
            return 0

        lax.fori_loop(0, share, body, 0, unroll=4)


def make_pairs(tiles, levs):
    def flat(t, g):
        return t * levs + g

    def zh(t):
        return (t >> 3) & 1

    edge = []
    for t in range(tiles):
        e = (t + 1) % tiles if t & 1 else (t - 1) % tiles
        for g in range(levs):
            edge.append((flat(t, g), flat(e, g if zh(t) == zh(e) else levs - 1 - g)))
    far = [(flat(t, g), flat(t ^ 8, levs - 1 - g)) for t in range(tiles) for g in range(levs)]

    def tile_xor(k):
        return [(t, t ^ k) for t in range(tiles)]

    def lev_xor(k):
        return [(g, g ^ k) for g in range(levs)]

    return edge, far, tile_xor, lev_xor


def per_device(
    control, ensemble, loc_blocks, neighbours, vert_band, channel_weights, innovation, inv_error
):
    members, ldev, pdev = control.shape
    tiles = lax.axis_size("tile")
    levs = lax.axis_size("lev")
    lev = levs * ldev
    share = members // levs
    rows = share * lev
    norm = 1.0 / math.sqrt(members - 1)
    edge, far, tile_xor, lev_xor = make_pairs(tiles, levs)
    both = ("tile", "lev")
    tile_pos = lax.axis_index("tile").astype(jnp.int32)
    lev_pos = lax.axis_index("lev").astype(jnp.int32)
    mset = lev_pos ^ (3 * ((tile_pos >> 3) & 1))
    scal = jnp.stack([tile_pos, lev_pos, mset, mset])

    def swap_core(x):
        return lax.ppermute(x, "tile", tile_xor(1))

    def swap_edge(x):
        return lax.ppermute(x, both, edge)

    def shuffle(parts):
        return [parts[0]] + [lax.ppermute(parts[k], "lev", lev_xor(k)) for k in range(1, 4)]

    chunk = sds((share, ldev, pdev), BF16)
    eparts = call(pack_ens_kernel, [chunk] * 4, (scal, ensemble), 1)
    eparts = shuffle(eparts)
    d_own, x_core, x_edge, vw, vwt = call(
        densify_kernel,
        [
            sds((256, 256), BF16), sds((352, 256), BF16), sds((352, 256), BF16),
            sds((NS, lev, 128), F32), sds((NS, lev, 128), F32),
        ],
        (scal, neighbours, loc_blocks, inv_error, innovation, vert_band),
        2,
        [pltpu.VMEM((12, 128, 128), F32)],
    )
    wt_own = jnp.pad(channel_weights.T, ((0, 0), (0, pdev - channel_weights.shape[0])))
    packed = call(
        pack_ctl_kernel,
        [sds((share + 3, ldev, pdev), BF16)] * 4 + [sds((ldev, pdev), F32)],
        (scal, control, wt_own),
        1,
    )
    s0 = packed[4]
    x_edge = swap_edge(x_edge)
    x_core = swap_core(x_core)
    field = sds((share, levs, ldev, pdev), BF16)
    (e_own,) = call(assemble_kernel, [field], (scal, *eparts), 1)
    e_edge = swap_edge(e_own)
    e_core = swap_core(e_own)
    cparts = shuffle(packed[:4])

    umat = pltpu.VMEM((rows, pdev), F32)
    half = pltpu.VMEM((rows, pdev), BF16)
    full = pltpu.VMEM((share, levs, ldev, pdev), F32)
    obs = channel_weights.shape[0]
    mm = 2 * rows * pdev * pdev * 3

    def bind(fn, arg):
        def body(*refs):
            fn(arg, *refs)

        return body

    cm, hx_core, hx_oe, w, wt = call(
        bind(first_kernel, norm),
        [
            field, sds((obs, pdev), F32), sds((2 * obs, pdev), F32),
            sds((obs, 128), F32), sds((lev, 128), F32),
        ],
        (scal, *cparts, e_own, e_core, e_edge, d_own, x_core, x_edge, vw),
        1,
        [full, pltpu.VMEM((128, 128), F32), half, umat],
        mm,
    )

    def reduce_obs(core_msg, oe):
        got = swap_core(core_msg)
        mine = jnp.concatenate([oe[:obs] + got[:obs], oe[obs:]], axis=0)
        other = swap_edge(mine)
        tot = mine + jnp.concatenate([other[obs:], other[:obs]], axis=0)
        if core_msg.shape[0] > obs:
            tot = jnp.concatenate([tot, core_msg[obs:] + got[obs:]], axis=0)
        tot = tot + lax.ppermute(tot, "lev", lev_xor(1))
        tot = tot + lax.ppermute(tot, "lev", lev_xor(2))
        return tot, swap_core(tot[:obs])

    h1_oe, h1_core = reduce_obs(hx_core, hx_oe)
    outs = call(
        bind(second_kernel, norm),
        [chunk] * 4 + [sds((obs + 8, pdev), F32), sds((2 * obs, pdev), F32)],
        (
            scal, h1_oe, h1_core, inv_error, innovation, cm, e_own, e_core, e_edge,
            d_own, x_core, x_edge, vw, vwt, w, wt, s0,
        ),
        1,
        [full, half, umat],
        2 * mm,
    )
    hs, hd_core = reduce_obs(outs[4], outs[5])
    sums = call(
        sums_kernel,
        [sds((8, pdev), F32)],
        (hs, hd_core, h1_oe, h1_core, inv_error, innovation, x_core),
        0,
    )[0]
    aparts = shuffle(outs[:4])
    bparts = call(
        bind(third_kernel, norm),
        [chunk] * 4,
        (
            scal, hs, hd_core, inv_error, e_own, e_core, e_edge, d_own, x_core, x_edge,
            vwt, wt,
        ),
        1,
        [full, half, umat],
        mm,
    )
    bparts = shuffle(bparts)
    for k in (2, 6):
        sums = sums + lax.ppermute(sums, "tile", tile_xor(k))
    sums = sums + lax.ppermute(sums, both, far)
    for k in (16, 48):
        sums = sums + lax.ppermute(sums, "tile", tile_xor(k))
    whole = sds((members, ldev, pdev), F32)
    (grad_first,) = call(grad_first_kernel, [whole], (scal, control, *aparts), 1)
    count = float(members * lev * pdev * tiles)
    grad_second, costs = call(
        bind(grad_second_kernel, count),
        [whole, sds((8, 128), F32)],
        (scal, grad_first, *bparts, sums),
        1,
    )
    return grad_first, grad_second, costs[0:2, 0]


def solution(mesh):
    placed = (
        P(None, "lev", "tile"),
        P(None, "lev", "tile"),
        P("tile", None, None, None),
        P("tile", None),
        P(),
        P(None, "lev"),
        P(None, "tile"),
        P(None, "tile"),
    )
    return jax.shard_map(
        per_device,
        mesh=mesh,
        in_specs=placed,
        out_specs=(P(None, "lev", "tile"), P(None, "lev", "tile"), P()),
        check_vma=False,
    )
```

```python
import math

import jax
import jax.numpy as jnp
from jax import lax
from jax.experimental import pallas as pl
from jax.experimental.pallas import tpu as pltpu
from jax.sharding import PartitionSpec as P


HV = 4
NS = 2 * HV + 1
STEP = 0.5
F32 = jnp.float32
BF16 = jnp.bfloat16
VM = pl.BlockSpec(memory_space=pltpu.VMEM)
SM = pl.BlockSpec(memory_space=pltpu.SMEM)


def call(body, outs, args, scalars, scratch=(), flops=0, specs=None, out_specs=None):
    if specs is None:
        specs = [SM] * scalars + [VM] * (len(args) - scalars)
    if out_specs is None:
        out_specs = tuple(VM for _ in outs)
    moved = sum(a.size * a.dtype.itemsize for a in args)
    moved += sum(math.prod(o.shape) * jnp.dtype(o.dtype).itemsize for o in outs)
    return pl.pallas_call(
        body,
        out_shape=tuple(outs),
        in_specs=specs,
        out_specs=out_specs,
        scratch_shapes=list(scratch),
        cost_estimate=pl.CostEstimate(flops=flops, bytes_accessed=moved, transcendentals=0),
        compiler_params=pltpu.CompilerParams(vmem_limit_bytes=48 * 1024 * 1024),
    )(*args)


def sds(shape, dtype):
    return jax.ShapeDtypeStruct(shape, dtype)


def split3(x):
    hi = x.astype(BF16)
    rest = x - hi.astype(F32)
    mid = rest.astype(BF16)
    lo = (rest - mid.astype(F32)).astype(BF16)
    return hi, mid, lo


def join3(hi, mid, lo):
    return (hi.astype(F32) + mid.astype(F32)) + lo.astype(F32)


def pack_ens_kernel(scal, ens, *refs):
    outs, sems = refs[:4], refs[4]
    share = outs[0].shape[0]
    copies = [
        pltpu.make_async_copy(
            ens.at[pl.ds(share * (scal[2] ^ k), share)], outs[k], sems.at[k]
        )
        for k in range(4)
    ]
    for c in copies:
        c.start()
    for c in copies:
        c.wait()


def pack_ctl_kernel(scal, ctl, wt, *outs):
    share = outs[0].shape[0] - 3
    parts = split3(wt[...])
    for k in range(4):
        outs[k][pl.ds(0, share)] = ctl[pl.ds(share * (scal[2] ^ k), share)].astype(BF16)
        for i in range(3):
            outs[k][share + i] = parts[i]
    sq = jnp.zeros(outs[4].shape, F32)

    def body(m, acc):
        v = ctl[m]
        return acc + v * v

    outs[4][...] = lax.fori_loop(0, ctl.shape[0], body, sq, unroll=4)


def densify_kernel(scal, nb, loc, inv, inn, vb, d_own, x_core, x_edge, vw, vwt, acc):
    tile = scal[0]
    core_rel = 2 - 2 * (tile & 1)
    acc[...] = jnp.zeros(acc.shape, F32)
    for b in range(2):
        for j in range(loc.shape[1]):
            n = nb[b, j]
            rel = ((n >> 1) - tile + 65) & 63
            role = jnp.where(rel == 1, 0, jnp.where(rel == core_rel, 1, 2))
            slot = b * 6 + role * 2 + (n & 1)
            acc[slot] = acc[slot] + loc[b, j].astype(F32)
    for role, out in enumerate((d_own, x_core, x_edge)):
        for b in range(2):
            for h in range(2):
                out[128 * b : 128 * b + 128, 128 * h : 128 * h + 128] = acc[
                    b * 6 + role * 2 + h
                ].astype(BF16)
    for out in (x_core, x_edge):
        for i, v in enumerate(split3(inv[...]) + split3(inn[...])):
            out[256 + 16 * i : 272 + 16 * i, :] = v
    lev = vb.shape[0]
    row = lax.broadcasted_iota(jnp.int32, (lev, 128), 0)
    for s in range(NS):
        col = jnp.broadcast_to(vb[:, s : s + 1], (lev, 128))
        src = row + (s - HV)
        vw[s] = jnp.where((src >= 0) & (src < lev), col, 0.0)
        src = row + (HV - s)
        moved = pltpu.roll(col, (s - HV) % lev, 0)
        vwt[s] = jnp.where((src >= 0) & (src < lev), moved, 0.0)


def assemble_kernel(scal, e0, e1, e2, e3, out):
    for k, e in enumerate((e0, e1, e2, e3)):
        out[:, scal[1] ^ k] = e[...]


def forward_part(src, vw, avb, umat, ens3, dmats, w, hxs, norm):
    ms = src.shape[0]
    lev = 32

    def smooth(m, _):
        block = src[m].reshape(lev, 256)
        cols = []
        for h in range(2):
            a = block[:, 128 * h : 128 * h + 128]
            tot = vw[HV] * a
            for s in range(NS):
                if s != HV:
                    tot = tot + vw[s] * pltpu.roll(a, (HV - s) % lev, 0)
            cols.append(tot)
        avb[pl.ds(pl.multiple_of(lev * m, lev), lev), :] = jnp.concatenate(cols, axis=1).astype(
            BF16
        )
        return 0

    lax.fori_loop(0, ms, smooth, 0)
    for ens, d, hx in zip(ens3, dmats, hxs):
        umat[...] = lax.dot_general(
            avb[...], d, (((1,), (1,)), ((), ())), preferred_element_type=F32
        )

        def member(m, acc):
            e = ens[m].astype(F32).reshape(lev, 256)
            return acc + e * umat[pl.ds(pl.multiple_of(lev * m, lev), lev), :]

        dx = lax.fori_loop(0, ms, member, jnp.zeros((lev, 256), F32), unroll=2)
        hx(
            jnp.dot(
                w[:, 0:lev], dx * norm, precision=lax.Precision.HIGHEST, preferred_element_type=F32
            )
        )


def adjoint_part(qs, wt, vwt, ens3, dmats, ua, umat, out, norm):
    ms = out.shape[0]
    lev = 32
    for r, (q, ens, d) in enumerate(zip(qs, ens3, dmats)):
        dxa = (
            jnp.dot(
                wt[:, 0:16], q, precision=lax.Precision.HIGHEST, preferred_element_type=F32
            )
            * norm
        )

        def member(m, _):
            e = ens[m].astype(F32).reshape(lev, 256)
            ua[pl.ds(pl.multiple_of(lev * m, lev), lev), :] = (e * dxa).astype(BF16)
            return 0

        lax.fori_loop(0, ms, member, 0, unroll=2)
        part = jnp.dot(ua[...], d, preferred_element_type=F32)
        if r == 0:
            umat[...] = part
        else:
            umat[...] = umat[...] + part

    def spread(m, _):
        block = umat[pl.ds(pl.multiple_of(lev * m, lev), lev), :]
        cols = []
        for h in range(2):
            a = block[:, 128 * h : 128 * h + 128]
            tot = vwt[HV] * a
            for s in range(NS):
                if s != HV:
                    tot = tot + vwt[s] * pltpu.roll(a, (s - HV) % lev, 0)
            cols.append(tot)
        out[m] = jnp.concatenate(cols, axis=1).reshape(4, 8, 256)
        return 0

    lax.fori_loop(0, ms, spread, 0)


def dmats_of(d_own, x_core, x_edge):
    return d_own[...], x_core[0:256, :], x_edge[0:256, :]


def obs_of(x):
    return (
        join3(x[256:272, :], x[272:288, :], x[288:304, :]),
        join3(x[304:320, :], x[320:336, :], x[336:352, :]),
    )


def first_kernel(
    norm, scal, c0, c1, c2, c3, e_own, e_core, e_edge, d_own, x_core, x_edge, vw,
    cm, hx_core, hx_oe, w, wt, src, wsq, avb, umat,
):
    share = src.shape[0]
    wsq[...] = jnp.zeros(wsq.shape, F32)
    for k, c in enumerate((c0, c1, c2, c3)):
        group = scal[1] ^ k
        val = c[pl.ds(0, share)]
        cm[:, group] = val
        src[:, group] = val.astype(F32)
        wsq[pl.ds(pl.multiple_of(8 * group, 8), 8), :] = join3(
            c[share], c[share + 1], c[share + 2]
        )[:, 0:128]
    w[...] = wsq[...].T[0:16, :]
    wt[...] = wsq[0:32, :]

    def put_own(v):
        hx_oe[0:16, :] = v

    def put_core(v):
        hx_core[...] = v

    def put_edge(v):
        hx_oe[16:32, :] = v

    forward_part(
        src, vw, avb, umat, (e_own, e_core, e_edge), dmats_of(d_own, x_core, x_edge), w,
        (put_own, put_core, put_edge), norm,
    )


def second_kernel(
    norm, scal, h_oe, h_core, inv, inn, cm, e_own, e_core, e_edge, d_own, x_core, x_edge,
    vw, vwt, w, wt, s0, a0, a1, a2, a3, hx_core, hx_oe, adj, ua, umat,
):
    share = adj.shape[0]
    ic, yc = obs_of(x_core)
    ie, ye = obs_of(x_edge)
    qs = (
        inv[...] * (h_oe[0:16, :] - inn[...]),
        ic * (h_core[...] - yc),
        ie * (h_oe[16:32, :] - ye),
    )
    ens3 = (e_own, e_core, e_edge)
    dmats = dmats_of(d_own, x_core, x_edge)
    adjoint_part(qs, wt, vwt, ens3, dmats, ua, umat, adj, norm)
    for k, a in enumerate((a0, a1, a2, a3)):
        a[...] = adj[:, scal[1] ^ k].astype(BF16)

    def total(m, carry):
        gg, cg = carry
        c = cm[m].astype(F32)
        g = c + adj[m]
        adj[m] = g
        return gg + jnp.sum(g * g, axis=0), cg + jnp.sum(c * g, axis=0)

    zero = jnp.zeros((8, 256), F32)
    gg, cg = lax.fori_loop(0, share, total, (zero, zero))

    def put_own(v):
        hx_oe[0:16, :] = v

    def put_core(v):
        hx_core[0:16, :] = v

    def put_edge(v):
        hx_oe[16:32, :] = v

    forward_part(
        adj, vw, ua, umat, ens3, dmats, w, (put_own, put_core, put_edge), norm
    )
    hx_core[16:24, :] = jnp.zeros((8, 256), F32)
    hx_core[16:17, :] = jnp.sum(s0[...], axis=0, keepdims=True)
    hx_core[17:18, :] = jnp.sum(gg, axis=0, keepdims=True)
    hx_core[18:19, :] = jnp.sum(cg, axis=0, keepdims=True)


def sums_kernel(hs, h_core, h1_oe, h1_core, inv, inn, x_core, out):
    ic, yc = obs_of(x_core)

    def rows(h1, i, y, d):
        diff = h1 - y
        q = i * diff
        return [
            jnp.sum(q * diff, axis=0, keepdims=True),
            jnp.sum(q * d, axis=0, keepdims=True),
            jnp.sum(i * d * d, axis=0, keepdims=True),
        ]

    own = rows(h1_oe[0:16, :], inv[...], inn[...], hs[0:16, :])
    core = rows(h1_core[...], ic, yc, h_core[...])
    out[...] = hs[32:40, :]
    for i in range(3):
        out[3 + i : 4 + i, :] = own[i] + core[i]


def third_kernel(
    norm, scal, h_oe, h_core, inv, e_own, e_core, e_edge, d_own, x_core, x_edge,
    vwt, wt, a0, a1, a2, a3, adj, ua, umat,
):
    ic, _ = obs_of(x_core)
    ie, _ = obs_of(x_edge)
    qs = (inv[...] * h_oe[0:16, :], ic * h_core[...], ie * h_oe[16:32, :])
    adjoint_part(
        qs, wt, vwt, (e_own, e_core, e_edge), dmats_of(d_own, x_core, x_edge), ua, umat, adj,
        norm,
    )
    for k, a in enumerate((a0, a1, a2, a3)):
        a[...] = adj[:, scal[1] ^ k].astype(BF16)


def grad_first_kernel(scal, ctl, a0, a1, a2, a3, out):
    share = a0.shape[0]
    for k, a in enumerate((a0, a1, a2, a3)):
        at = pl.ds(share * (scal[2] ^ k), share)
        out[at] = ctl[at] + a[...].astype(F32)


def grad_second_kernel(
    count, scal, ctl, a0, a1, a2, a3, b0, b1, b2, b3, sums, out, costs
):
    tot = jnp.sum(sums[...], axis=1, keepdims=True)
    cc, gg, cg = tot[0:1], tot[1:2], tot[2:3]
    dd, qd, rd = tot[3:4], tot[4:5], tot[5:6]
    tau = STEP / jnp.sqrt(gg / count + 1e-06)
    first = (0.5 * cc + 0.5 * dd) / count
    second = 0.5 * (cc - 2.0 * tau * cg + tau * tau * gg) + 0.5 * (
        dd - 2.0 * tau * qd + tau * tau * rd
    )
    costs[0] = first[0, 0]
    costs[1] = (second / count)[0, 0]
    tb = jnp.broadcast_to(tau, (8, 256))
    share = a0.shape[0]
    for k, (a, b) in enumerate(zip((a0, a1, a2, a3), (b0, b1, b2, b3))):

        def body(m, _, a=a, b=b, k=k):
            at = share * (scal[2] ^ k) + m
            g = ctl[at] + a[m].astype(F32)
            out[at] = g - tb * (g + b[m].astype(F32))
            return 0

        lax.fori_loop(0, share, body, 0, unroll=4)


def make_pairs(tiles, levs):
    def flat(t, g):
        return t * levs + g

    def zh(t):
        return (t >> 3) & 1

    edge = []
    for t in range(tiles):
        e = (t + 1) % tiles if t & 1 else (t - 1) % tiles
        for g in range(levs):
            edge.append((flat(t, g), flat(e, g if zh(t) == zh(e) else g ^ 2)))
    far = [(flat(t, g), flat(t ^ 8, g ^ 2)) for t in range(tiles) for g in range(levs)]

    def tile_xor(k):
        return [(t, t ^ k) for t in range(tiles)]

    def lev_xor(k):
        return [(g, g ^ k) for g in range(levs)]

    return edge, far, tile_xor, lev_xor


def per_device(
    control, ensemble, loc_blocks, neighbours, vert_band, channel_weights, innovation, inv_error
):
    members, ldev, pdev = control.shape
    tiles = lax.axis_size("tile")
    levs = lax.axis_size("lev")
    lev = levs * ldev
    share = members // levs
    rows = share * lev
    norm = 1.0 / math.sqrt(members - 1)
    edge, far, tile_xor, lev_xor = make_pairs(tiles, levs)
    both = ("tile", "lev")
    tile_pos = lax.axis_index("tile").astype(jnp.int32)
    lev_pos = lax.axis_index("lev").astype(jnp.int32)
    mset = lev_pos ^ (2 * ((tile_pos >> 3) & 1))
    scal = jnp.stack([tile_pos, lev_pos, mset, mset])

    def swap_core(x):
        return lax.ppermute(x, "tile", tile_xor(1))

    def swap_edge(x):
        return lax.ppermute(x, both, edge)

    def shuffle(parts):
        return [parts[0]] + [
            lax.ppermute(parts[k], "lev", lev_xor(k)) for k in range(1, 4)
        ]

    def sum4(x, axis, pairs, steps):
        one, two, three = (
            lax.ppermute(x, axis, pairs(k)) for k in steps
        )
        return (x + one) + (two + three)

    chunk = sds((share, ldev, pdev), BF16)
    eparts = call(
        pack_ens_kernel, [chunk] * 4, (scal, ensemble), 1,
        [pltpu.SemaphoreType.DMA((4,))],
        specs=[SM, pl.BlockSpec(memory_space=pltpu.HBM)],
    )
    eparts = shuffle(eparts)
    d_own, x_core, x_edge, vw, vwt = call(
        densify_kernel,
        [
            sds((256, 256), BF16), sds((352, 256), BF16), sds((352, 256), BF16),
            sds((NS, lev, 128), F32), sds((NS, lev, 128), F32),
        ],
        (scal, neighbours, loc_blocks, inv_error, innovation, vert_band),
        2,
        [pltpu.VMEM((12, 128, 128), F32)],
    )
    wt_own = jnp.pad(channel_weights.T, ((0, 0), (0, pdev - channel_weights.shape[0])))
    packed = call(
        pack_ctl_kernel,
        [sds((share + 3, ldev, pdev), BF16)] * 4 + [sds((ldev, pdev), F32)],
        (scal, control, wt_own),
        1,
    )
    s0 = packed[4]
    x_edge = swap_edge(x_edge)
    x_core = swap_core(x_core)
    field = sds((share, levs, ldev, pdev), BF16)
    (e_own,) = call(assemble_kernel, [field], (scal, *eparts), 1)
    e_edge = swap_edge(e_own)
    e_core = swap_core(e_own)
    cparts = shuffle(packed[:4])

    umat = pltpu.VMEM((rows, pdev), F32)
    half = pltpu.VMEM((rows, pdev), BF16)
    full = pltpu.VMEM((share, levs, ldev, pdev), F32)
    obs = channel_weights.shape[0]
    mm = 2 * rows * pdev * pdev * 3

    def bind(fn, arg):
        def body(*refs):
            fn(arg, *refs)

        return body

    cm, hx_core, hx_oe, w, wt = call(
        bind(first_kernel, norm),
        [
            field, sds((obs, pdev), F32), sds((2 * obs, pdev), F32),
            sds((obs, 128), F32), sds((lev, 128), F32),
        ],
        (scal, *cparts, e_own, e_core, e_edge, d_own, x_core, x_edge, vw),
        1,
        [full, pltpu.VMEM((128, 128), F32), half, umat],
        mm,
    )

    def reduce_obs(core_msg, oe):
        got = swap_core(core_msg)
        mine = jnp.concatenate([oe[:obs] + got[:obs], oe[obs:]], axis=0)
        other = swap_edge(mine)
        tot = mine + jnp.concatenate([other[obs:], other[:obs]], axis=0)
        if core_msg.shape[0] > obs:
            extra = core_msg[obs:] + got[obs:]
            tot = jnp.concatenate([tot, extra], axis=0)
        tot = sum4(tot, "lev", lev_xor, (1, 2, 3))
        return tot, swap_core(tot[:obs])

    h1_oe, h1_core = reduce_obs(hx_core, hx_oe)
    outs = call(
        bind(second_kernel, norm),
        [chunk] * 4 + [sds((obs + 8, pdev), F32), sds((2 * obs, pdev), F32)],
        (
            scal, h1_oe, h1_core, inv_error, innovation, cm, e_own, e_core, e_edge,
            d_own, x_core, x_edge, vw, vwt, w, wt, s0,
        ),
        1,
        [full, half, umat],
        2 * mm,
    )
    aparts = shuffle(outs[:4])
    hs, hd_core = reduce_obs(outs[4], outs[5])
    sums = call(
        sums_kernel,
        [sds((8, pdev), F32)],
        (hs, hd_core, h1_oe, h1_core, inv_error, innovation, x_core),
        0,
    )[0]
    bparts = call(
        bind(third_kernel, norm),
        [chunk] * 4,
        (
            scal, hs, hd_core, inv_error, e_own, e_core, e_edge, d_own, x_core, x_edge,
            vwt, wt,
        ),
        1,
        [full, half, umat],
        mm,
    )
    bparts = shuffle(bparts)
    sums = sum4(sums, "tile", tile_xor, (2, 4, 6))
    sums = sums + lax.ppermute(sums, both, far)
    sums = sum4(sums, "tile", tile_xor, (16, 32, 48))
    whole = sds((members, ldev, pdev), F32)
    (grad_first,) = call(grad_first_kernel, [whole], (scal, control, *aparts), 1)
    count = float(members * lev * pdev * tiles)
    grad_second, costs = call(
        bind(grad_second_kernel, count),
        [whole, sds((2,), F32)],
        (scal, control, *aparts, *bparts, sums),
        1,
        out_specs=(VM, SM),
    )
    return grad_first, grad_second, costs


def solution(mesh):
    placed = (
        P(None, "lev", "tile"),
        P(None, "lev", "tile"),
        P("tile", None, None, None),
        P("tile", None),
        P(),
        P(None, "lev"),
        P(None, "tile"),
        P(None, "tile"),
    )
    return jax.shard_map(
        per_device,
        mesh=mesh,
        in_specs=placed,
        out_specs=(P(None, "lev", "tile"), P(None, "lev", "tile"), P()),
        check_vma=False,
    )
```

```python
import math

import jax
import jax.numpy as jnp
from jax import lax
from jax.experimental import pallas as pl
from jax.experimental.pallas import tpu as pltpu
from jax.sharding import PartitionSpec as P


HV = 4
NS = 2 * HV + 1
STEP = 0.5
GRP = 160
F32 = jnp.float32
BF16 = jnp.bfloat16
VM = pl.BlockSpec(memory_space=pltpu.VMEM)
SM = pl.BlockSpec(memory_space=pltpu.SMEM)


def call(body, outs, args, scalars, scratch=(), flops=0, specs=None, out_specs=None):
    if specs is None:
        specs = [SM] * scalars + [VM] * (len(args) - scalars)
    if out_specs is None:
        out_specs = tuple(VM for _ in outs)
    moved = sum(a.size * a.dtype.itemsize for a in args)
    moved += sum(math.prod(o.shape) * jnp.dtype(o.dtype).itemsize for o in outs)
    return pl.pallas_call(
        body,
        out_shape=tuple(outs),
        in_specs=specs,
        out_specs=out_specs,
        scratch_shapes=list(scratch),
        cost_estimate=pl.CostEstimate(flops=flops, bytes_accessed=moved, transcendentals=0),
        compiler_params=pltpu.CompilerParams(vmem_limit_bytes=48 * 1024 * 1024),
    )(*args)


def sds(shape, dtype):
    return jax.ShapeDtypeStruct(shape, dtype)


def split3(x):
    hi = x.astype(BF16)
    rest = x - hi.astype(F32)
    mid = rest.astype(BF16)
    lo = (rest - mid.astype(F32)).astype(BF16)
    return hi, mid, lo


def join3(hi, mid, lo):
    return (hi.astype(F32) + mid.astype(F32)) + lo.astype(F32)


def pack_ens_kernel(scal, ens, *refs):
    outs, sems = refs[:4], refs[4]
    share = outs[0].shape[0]
    copies = [
        pltpu.make_async_copy(
            ens.at[pl.ds(share * (scal[2] ^ k), share)], outs[k], sems.at[k]
        )
        for k in range(4)
    ]
    for c in copies:
        c.start()
    for c in copies:
        c.wait()


def pack_ctl_kernel(scal, ctl, wt, *outs):
    share = outs[0].shape[0] - 3
    parts = split3(wt[...])
    for k in range(4):
        outs[k][pl.ds(0, share)] = ctl[pl.ds(share * (scal[2] ^ k), share)].astype(BF16)
        for i in range(3):
            outs[k][share + i] = parts[i]
    sq = jnp.zeros(outs[4].shape, F32)

    def body(m, acc):
        v = ctl[m]
        return acc + v * v

    outs[4][...] = lax.fori_loop(0, ctl.shape[0], body, sq, unroll=4)


def densify_kernel(
    scal, nb, loc_hbm, inv_hbm, inn_hbm, band, d_own, x_core, x_edge, bands, acc, loc, obs, mat,
    sems,
):
    copies = [
        pltpu.make_async_copy(loc_hbm.at[0], loc.at[0], sems.at[0]),
        pltpu.make_async_copy(loc_hbm.at[1], loc.at[1], sems.at[1]),
        pltpu.make_async_copy(inv_hbm, obs.at[0], sems.at[2]),
        pltpu.make_async_copy(inn_hbm, obs.at[1], sems.at[3]),
    ]
    for c in copies:
        c.start()
    row = lax.broadcasted_iota(jnp.int32, (256, 256), 0)
    col = lax.broadcasted_iota(jnp.int32, (256, 256), 1)
    shift = row - col
    same = (row >> 5) == (col >> 5)
    tot = jnp.zeros((256, 256), F32)
    for s in range(NS):
        tot = jnp.where(same & (shift == s - HV), band[s : s + 1, :], tot)
    mat[...] = tot
    back = mat[...]
    fwd = mat[...].T
    for i, m in enumerate((fwd, back)):
        hi = m.astype(BF16)
        bands[2 * i] = hi[0:GRP, 0:GRP]
        bands[2 * i + 1] = (m - hi.astype(F32)).astype(BF16)[0:GRP, 0:GRP]
    tile = scal[0]
    core_rel = 2 - 2 * (tile & 1)
    acc[...] = jnp.zeros(acc.shape, F32)
    for b in range(2):
        copies[b].wait()
        for j in range(loc.shape[1]):
            n = nb[b, j]
            rel = ((n >> 1) - tile + 65) & 63
            role = jnp.where(rel == 1, 0, jnp.where(rel == core_rel, 1, 2))
            slot = b * 6 + role * 2 + (n & 1)
            acc[slot] = acc[slot] + loc[b, j].astype(F32)
    for role, out in enumerate((d_own, x_core, x_edge)):
        for b in range(2):
            for h in range(2):
                out[128 * b : 128 * b + 128, 128 * h : 128 * h + 128] = acc[
                    b * 6 + role * 2 + h
                ].astype(BF16)
    copies[2].wait()
    copies[3].wait()
    for out in (x_core, x_edge):
        for i, v in enumerate(split3(obs[0]) + split3(obs[1])):
            out[256 + 16 * i : 272 + 16 * i, :] = v


def assemble_kernel(scal, e0, e1, e2, e3, out):
    for k, e in enumerate((e0, e1, e2, e3)):
        out[:, scal[1] ^ k] = e[...]


def band_apply(mats, x, exact):
    hi, lo = mats

    def mul(a, b):
        return jnp.dot(a, b, preferred_element_type=F32)

    if exact:
        return mul(hi, x) + mul(lo, x)
    xh = x.astype(BF16)
    xl = (x - xh.astype(F32)).astype(BF16)
    return mul(hi, xh) + (mul(lo, xh) + mul(hi, xl))


def forward_part(src, exact, mats, avb, umat, ens3, dmats, w, hxs, norm):
    rows = avb.shape[0]
    lev = 32
    ms = rows // lev
    for r in range(0, rows, GRP):
        avb[r : r + GRP, :] = band_apply(mats, src(r), exact).astype(BF16)
    for ens, d, hx in zip(ens3, dmats, hxs):
        umat[...] = lax.dot_general(
            avb[...], d, (((1,), (1,)), ((), ())), preferred_element_type=F32
        )

        def member(m, acc):
            e = ens[m].astype(F32).reshape(lev, 256)
            return acc + e * umat[pl.ds(pl.multiple_of(lev * m, lev), lev), :]

        dx = lax.fori_loop(0, ms, member, jnp.zeros((lev, 256), F32), unroll=4)
        hx(
            jnp.dot(
                w[:, 0:lev], dx * norm, precision=lax.Precision.HIGHEST, preferred_element_type=F32
            )
        )


def adjoint_part(qs, wt, mats, ens3, dmats, ua, umat, out, norm):
    ms = out.shape[0]
    lev = 32
    for r, (q, ens, d) in enumerate(zip(qs, ens3, dmats)):
        dxa = (
            jnp.dot(
                wt[:, 0:16], q, precision=lax.Precision.HIGHEST, preferred_element_type=F32
            )
            * norm
        )

        def member(m, _):
            e = ens[m].astype(F32).reshape(lev, 256)
            ua[pl.ds(pl.multiple_of(lev * m, lev), lev), :] = (e * dxa).astype(BF16)
            return 0

        lax.fori_loop(0, ms, member, 0, unroll=4)
        part = jnp.dot(ua[...], d, preferred_element_type=F32)
        if r == 0:
            umat[...] = part
        else:
            umat[...] = umat[...] + part
    five = GRP // lev
    for i in range(0, ms, five):
        got = band_apply(mats, umat[lev * i : lev * i + GRP, :], False)
        out[i : i + five] = got.reshape(five, 4, 8, 256)


def dmats_of(d_own, x_core, x_edge):
    return d_own[...], x_core[0:256, :], x_edge[0:256, :]


def obs_of(x):
    return (
        join3(x[256:272, :], x[272:288, :], x[288:304, :]),
        join3(x[304:320, :], x[320:336, :], x[336:352, :]),
    )


def first_kernel(
    norm, scal, c0, c1, c2, c3, e_own, e_core, e_edge, d_own, x_core, x_edge, bands,
    cm, hx_core, hx_oe, w, wt, src, wsq, avb, umat,
):
    share = src.shape[0]
    wsq[...] = jnp.zeros(wsq.shape, F32)
    for k, c in enumerate((c0, c1, c2, c3)):
        group = scal[1] ^ k
        val = c[pl.ds(0, share)]
        cm[:, group] = val
        src[:, group] = val.astype(F32)
        wsq[pl.ds(pl.multiple_of(8 * group, 8), 8), :] = join3(
            c[share], c[share + 1], c[share + 2]
        )[:, 0:128]
    w[...] = wsq[...].T[0:16, :]
    wt[...] = wsq[0:32, :]

    def put_own(v):
        hx_oe[0:16, :] = v

    def put_core(v):
        hx_core[...] = v

    def put_edge(v):
        hx_oe[16:32, :] = v

    def rows_of(r):
        five = GRP // 32
        return src[r // 32 : r // 32 + five].reshape(GRP, 256).astype(BF16)

    forward_part(
        rows_of, True, (bands[0], bands[1]), avb, umat, (e_own, e_core, e_edge),
        dmats_of(d_own, x_core, x_edge), w, (put_own, put_core, put_edge), norm,
    )


def second_kernel(
    norm, scal, h_oe, h_core, inv, inn, cm, e_own, e_core, e_edge, d_own, x_core, x_edge,
    bands, w, wt, s0, a0, a1, a2, a3, hx_core, hx_oe, adj, ua, umat,
):
    share = adj.shape[0]
    ic, yc = obs_of(x_core)
    ie, ye = obs_of(x_edge)
    qs = (
        inv[...] * (h_oe[0:16, :] - inn[...]),
        ic * (h_core[...] - yc),
        ie * (h_oe[16:32, :] - ye),
    )
    ens3 = (e_own, e_core, e_edge)
    dmats = dmats_of(d_own, x_core, x_edge)
    adjoint_part(qs, wt, (bands[2], bands[3]), ens3, dmats, ua, umat, adj, norm)
    for k, a in enumerate((a0, a1, a2, a3)):
        a[...] = adj[:, scal[1] ^ k].astype(BF16)

    def total(m, carry):
        gg, cg = carry
        c = cm[m].astype(F32)
        g = c + adj[m]
        adj[m] = g
        return gg + jnp.sum(g * g, axis=0), cg + jnp.sum(c * g, axis=0)

    zero = jnp.zeros((8, 256), F32)
    gg, cg = lax.fori_loop(0, share, total, (zero, zero))

    def put_own(v):
        hx_oe[0:16, :] = v

    def put_core(v):
        hx_core[0:16, :] = v

    def put_edge(v):
        hx_oe[16:32, :] = v

    def rows_of(r):
        five = GRP // 32
        return adj[r // 32 : r // 32 + five].reshape(GRP, 256)

    forward_part(
        rows_of, False, (bands[0], bands[1]), ua, umat, ens3, dmats, w,
        (put_own, put_core, put_edge), norm,
    )
    hx_core[16:24, :] = jnp.zeros((8, 256), F32)
    hx_core[16:17, :] = jnp.sum(s0[...], axis=0, keepdims=True)
    hx_core[17:18, :] = jnp.sum(gg, axis=0, keepdims=True)
    hx_core[18:19, :] = jnp.sum(cg, axis=0, keepdims=True)


def sums_kernel(hs, h_core, h1_oe, h1_core, inv, inn, x_core, out):
    ic, yc = obs_of(x_core)

    def rows(h1, i, y, d):
        diff = h1 - y
        q = i * diff
        return [
            jnp.sum(q * diff, axis=0, keepdims=True),
            jnp.sum(q * d, axis=0, keepdims=True),
            jnp.sum(i * d * d, axis=0, keepdims=True),
        ]

    own = rows(h1_oe[0:16, :], inv[...], inn[...], hs[0:16, :])
    core = rows(h1_core[...], ic, yc, h_core[...])
    out[...] = hs[32:40, :]
    for i in range(3):
        out[3 + i : 4 + i, :] = own[i] + core[i]


def third_kernel(
    norm, scal, h_oe, h_core, inv, e_own, e_core, e_edge, d_own, x_core, x_edge,
    bands, wt, a0, a1, a2, a3, adj, ua, umat,
):
    ic, _ = obs_of(x_core)
    ie, _ = obs_of(x_edge)
    qs = (inv[...] * h_oe[0:16, :], ic * h_core[...], ie * h_oe[16:32, :])
    adjoint_part(
        qs, wt, (bands[2], bands[3]), (e_own, e_core, e_edge), dmats_of(d_own, x_core, x_edge),
        ua, umat, adj, norm,
    )
    for k, a in enumerate((a0, a1, a2, a3)):
        a[...] = adj[:, scal[1] ^ k].astype(BF16)


def grad_first_kernel(scal, ctl, a0, a1, a2, a3, out, buf, sems):
    share = a0.shape[0]
    copies = []
    for k, a in enumerate((a0, a1, a2, a3)):
        at = pl.ds(share * (scal[2] ^ k), share)
        buf[k] = ctl[at] + a[...].astype(F32)
        copies.append(pltpu.make_async_copy(buf.at[k], out.at[at], sems.at[k]))
        copies[k].start()
    for c in copies:
        c.wait()


def grad_second_kernel(
    count, scal, ctl, a0, a1, a2, a3, b0, b1, b2, b3, sums, out, costs, buf, sems
):
    tot = jnp.sum(sums[...], axis=1, keepdims=True)
    cc, gg, cg = tot[0:1], tot[1:2], tot[2:3]
    dd, qd, rd = tot[3:4], tot[4:5], tot[5:6]
    tau = STEP / jnp.sqrt(gg / count + 1e-06)
    first = (0.5 * cc + 0.5 * dd) / count
    second = 0.5 * (cc - 2.0 * tau * cg + tau * tau * gg) + 0.5 * (
        dd - 2.0 * tau * qd + tau * tau * rd
    )
    tb = jnp.broadcast_to(tau, (8, 256))
    share = a0.shape[0]
    copies = []
    for k, (a, b) in enumerate(zip((a0, a1, a2, a3), (b0, b1, b2, b3))):
        base = share * (scal[2] ^ k)

        def body(m, _, a=a, b=b, k=k, base=base):
            g = ctl[base + m] + a[m].astype(F32)
            buf[k, m] = g - tb * (g + b[m].astype(F32))
            return 0

        lax.fori_loop(0, share, body, 0, unroll=5)
        copies.append(
            pltpu.make_async_copy(buf.at[k], out.at[pl.ds(base, share)], sems.at[k])
        )
        copies[k].start()
    costs[0] = first[0, 0]
    costs[1] = (second / count)[0, 0]
    for c in copies:
        c.wait()


def make_pairs(tiles, levs):
    def flat(t, g):
        return t * levs + g

    def zh(t):
        return (t >> 3) & 1

    edge = []
    for t in range(tiles):
        e = (t + 1) % tiles if t & 1 else (t - 1) % tiles
        for g in range(levs):
            edge.append((flat(t, g), flat(e, g if zh(t) == zh(e) else g ^ 2)))
    far = [(flat(t, g), flat(t ^ 8, g ^ 2)) for t in range(tiles) for g in range(levs)]

    def tile_xor(k):
        return [(t, t ^ k) for t in range(tiles)]

    def lev_xor(k):
        return [(g, g ^ k) for g in range(levs)]

    return edge, far, tile_xor, lev_xor


def per_device(
    control, ensemble, loc_blocks, neighbours, vert_band, channel_weights, innovation, inv_error
):
    members, ldev, pdev = control.shape
    tiles = lax.axis_size("tile")
    levs = lax.axis_size("lev")
    lev = levs * ldev
    share = members // levs
    rows = share * lev
    norm = 1.0 / math.sqrt(members - 1)
    edge, far, tile_xor, lev_xor = make_pairs(tiles, levs)
    both = ("tile", "lev")
    tile_pos = lax.axis_index("tile").astype(jnp.int32)
    lev_pos = lax.axis_index("lev").astype(jnp.int32)
    mset = lev_pos ^ (2 * ((tile_pos >> 3) & 1))
    scal = jnp.stack([tile_pos, lev_pos, mset, mset])

    def swap_core(x):
        return lax.ppermute(x, "tile", tile_xor(1))

    def swap_edge(x):
        return lax.ppermute(x, both, edge)

    def shuffle(parts):
        return [parts[0]] + [
            lax.ppermute(parts[k], "lev", lev_xor(k)) for k in range(1, 4)
        ]

    def sum4(x, axis, pairs, steps):
        one, two, three = (
            lax.ppermute(x, axis, pairs(k)) for k in steps
        )
        return (x + one) + (two + three)

    chunk = sds((share, ldev, pdev), BF16)
    hbm = pl.BlockSpec(memory_space=pltpu.HBM)

    def far_off(x):
        return pltpu.with_memory_space_constraint(x, pltpu.HBM)

    eparts = call(
        pack_ens_kernel, [chunk] * 4, (scal, far_off(ensemble)), 1,
        [pltpu.SemaphoreType.DMA((4,))],
        specs=[SM, hbm],
    )
    eparts = shuffle(eparts)
    band = jnp.tile(vert_band.T, (1, 8))
    d_own, x_core, x_edge, bands = call(
        densify_kernel,
        [
            sds((256, 256), BF16), sds((352, 256), BF16), sds((352, 256), BF16),
            sds((4, GRP, GRP), BF16),
        ],
        (
            scal, neighbours, far_off(loc_blocks), far_off(inv_error), far_off(innovation), band,
        ),
        2,
        [
            pltpu.VMEM((12, 128, 128), F32), pltpu.VMEM(loc_blocks.shape, BF16),
            pltpu.VMEM((2,) + inv_error.shape, F32), pltpu.VMEM((256, 256), F32),
            pltpu.SemaphoreType.DMA((4,)),
        ],
        specs=[SM, SM, hbm, hbm, hbm, VM],
    )
    wt_own = jnp.pad(channel_weights.T, ((0, 0), (0, pdev - channel_weights.shape[0])))
    packed = call(
        pack_ctl_kernel,
        [sds((share + 3, ldev, pdev), BF16)] * 4 + [sds((ldev, pdev), F32)],
        (scal, control, wt_own),
        1,
    )
    s0 = packed[4]
    x_edge = swap_edge(x_edge)
    x_core = swap_core(x_core)
    field = sds((share, levs, ldev, pdev), BF16)
    (e_own,) = call(assemble_kernel, [field], (scal, *eparts), 1)
    e_edge = swap_edge(e_own)
    e_core = swap_core(e_own)
    cparts = shuffle(packed[:4])

    umat = pltpu.VMEM((rows, pdev), F32)
    half = pltpu.VMEM((rows, pdev), BF16)
    full = pltpu.VMEM((share, levs, ldev, pdev), F32)
    obs = channel_weights.shape[0]
    mm = 2 * rows * pdev * pdev * 3

    def bind(fn, arg):
        def body(*refs):
            fn(arg, *refs)

        return body

    cm, hx_core, hx_oe, w, wt = call(
        bind(first_kernel, norm),
        [
            field, sds((obs, pdev), F32), sds((2 * obs, pdev), F32),
            sds((obs, 128), F32), sds((lev, 128), F32),
        ],
        (scal, *cparts, e_own, e_core, e_edge, d_own, x_core, x_edge, bands),
        1,
        [full, pltpu.VMEM((128, 128), F32), half, umat],
        mm,
    )

    def reduce_obs(core_msg, oe):
        got = swap_core(core_msg)
        mine = jnp.concatenate([oe[:obs] + got[:obs], oe[obs:]], axis=0)
        other = swap_edge(mine)
        tot = mine + jnp.concatenate([other[obs:], other[:obs]], axis=0)
        if core_msg.shape[0] > obs:
            extra = core_msg[obs:] + got[obs:]
            tot = jnp.concatenate([tot, extra], axis=0)
        tot = sum4(tot, "lev", lev_xor, (1, 2, 3))
        return tot, swap_core(tot[:obs])

    h1_oe, h1_core = reduce_obs(hx_core, hx_oe)
    outs = call(
        bind(second_kernel, norm),
        [chunk] * 4 + [sds((obs + 8, pdev), F32), sds((2 * obs, pdev), F32)],
        (
            scal, h1_oe, h1_core, inv_error, innovation, cm, e_own, e_core, e_edge,
            d_own, x_core, x_edge, bands, w, wt, s0,
        ),
        1,
        [full, half, umat],
        2 * mm,
    )
    aparts = shuffle(outs[:4])
    hs, hd_core = reduce_obs(outs[4], outs[5])
    sums = call(
        sums_kernel,
        [sds((8, pdev), F32)],
        (hs, hd_core, h1_oe, h1_core, inv_error, innovation, x_core),
        0,
    )[0]
    bparts = call(
        bind(third_kernel, norm),
        [chunk] * 4,
        (
            scal, hs, hd_core, inv_error, e_own, e_core, e_edge, d_own, x_core, x_edge,
            bands, wt,
        ),
        1,
        [full, half, umat],
        mm,
    )
    bparts = shuffle(bparts)
    sums = sum4(sums, "tile", tile_xor, (2, 4, 6))
    sums = sums + lax.ppermute(sums, both, far)
    sums = sum4(sums, "tile", tile_xor, (16, 32, 48))
    whole = sds((members, ldev, pdev), F32)
    anywhere = pl.BlockSpec(memory_space=pl.ANY)
    outbuf = [pltpu.VMEM((4, share, ldev, pdev), F32), pltpu.SemaphoreType.DMA((4,))]
    (grad_first,) = call(
        grad_first_kernel, [whole], (scal, control, *aparts), 1, outbuf,
        out_specs=(anywhere,),
    )
    count = float(members * lev * pdev * tiles)
    grad_second, costs = call(
        bind(grad_second_kernel, count),
        [whole, sds((2,), F32)],
        (scal, control, *aparts, *bparts, sums),
        1,
        outbuf,
        out_specs=(anywhere, SM),
    )
    return grad_first, grad_second, costs


def solution(mesh):
    placed = (
        P(None, "lev", "tile"),
        P(None, "lev", "tile"),
        P("tile", None, None, None),
        P("tile", None),
        P(),
        P(None, "lev"),
        P(None, "tile"),
        P(None, "tile"),
    )
    return jax.shard_map(
        per_device,
        mesh=mesh,
        in_specs=placed,
        out_specs=(P(None, "lev", "tile"), P(None, "lev", "tile"), P()),
        check_vma=False,
    )
```

```python
import math

import jax
import jax.numpy as jnp
from jax import lax
from jax.experimental import pallas as pl
from jax.experimental.pallas import tpu as pltpu
from jax.sharding import PartitionSpec as P


HV = 4
NS = 2 * HV + 1
STEP = 0.5
GRP = 160
F32 = jnp.float32
BF16 = jnp.bfloat16
VM = pl.BlockSpec(memory_space=pltpu.VMEM)
SM = pl.BlockSpec(memory_space=pltpu.SMEM)


def call(body, outs, args, scalars, scratch=(), flops=0, specs=None, out_specs=None):
    if specs is None:
        specs = [SM] * scalars + [VM] * (len(args) - scalars)
    if out_specs is None:
        out_specs = tuple(VM for _ in outs)
    moved = sum(a.size * a.dtype.itemsize for a in args)
    moved += sum(math.prod(o.shape) * jnp.dtype(o.dtype).itemsize for o in outs)
    return pl.pallas_call(
        body,
        out_shape=tuple(outs),
        in_specs=specs,
        out_specs=out_specs,
        scratch_shapes=list(scratch),
        cost_estimate=pl.CostEstimate(flops=flops, bytes_accessed=moved, transcendentals=0),
        compiler_params=pltpu.CompilerParams(vmem_limit_bytes=48 * 1024 * 1024),
    )(*args)


def sds(shape, dtype):
    return jax.ShapeDtypeStruct(shape, dtype)


def split3(x):
    hi = x.astype(BF16)
    rest = x - hi.astype(F32)
    mid = rest.astype(BF16)
    lo = (rest - mid.astype(F32)).astype(BF16)
    return hi, mid, lo


def join3(hi, mid, lo):
    return (hi.astype(F32) + mid.astype(F32)) + lo.astype(F32)


def pack_ens_kernel(scal, ens, *refs):
    outs, sems = refs[:4], refs[4]
    share = outs[0].shape[0]
    copies = [
        pltpu.make_async_copy(
            ens.at[pl.ds(share * (scal[2] ^ k), share)], outs[k], sems.at[k]
        )
        for k in range(4)
    ]
    for c in copies:
        c.start()
    for c in copies:
        c.wait()


def pack_ctl_kernel(scal, ctl, wt, *outs):
    share = outs[0].shape[0] - 3
    parts = split3(wt[...])
    for k in range(4):
        outs[k][pl.ds(0, share)] = ctl[pl.ds(share * (scal[2] ^ k), share)].astype(BF16)
        for i in range(3):
            outs[k][share + i] = parts[i]
    sq = jnp.zeros(outs[4].shape, F32)

    def body(m, acc):
        v = ctl[m]
        return acc + v * v

    outs[4][...] = lax.fori_loop(0, ctl.shape[0], body, sq, unroll=4)


def densify_kernel(
    scal, nb, loc_hbm, inv_hbm, inn_hbm, band, d_own, x_core, x_edge, bands, acc, loc, obs, mat,
    sems,
):
    copies = [
        pltpu.make_async_copy(loc_hbm.at[0], loc.at[0], sems.at[0]),
        pltpu.make_async_copy(loc_hbm.at[1], loc.at[1], sems.at[1]),
        pltpu.make_async_copy(inv_hbm, obs.at[0], sems.at[2]),
        pltpu.make_async_copy(inn_hbm, obs.at[1], sems.at[3]),
    ]
    for c in copies:
        c.start()
    row = lax.broadcasted_iota(jnp.int32, (256, 256), 0)
    col = lax.broadcasted_iota(jnp.int32, (256, 256), 1)
    shift = row - col
    same = (row >> 5) == (col >> 5)
    tot = jnp.zeros((256, 256), F32)
    for s in range(NS):
        tot = jnp.where(same & (shift == s - HV), band[s : s + 1, :], tot)
    mat[...] = tot
    back = mat[...]
    fwd = mat[...].T
    for i, m in enumerate((fwd, back)):
        hi = m.astype(BF16)
        bands[2 * i] = hi[0:GRP, 0:GRP]
        bands[2 * i + 1] = (m - hi.astype(F32)).astype(BF16)[0:GRP, 0:GRP]
    tile = scal[0]
    core_rel = 2 - 2 * (tile & 1)
    acc[...] = jnp.zeros(acc.shape, F32)
    for b in range(2):
        copies[b].wait()
        for j in range(loc.shape[1]):
            n = nb[b, j]
            rel = ((n >> 1) - tile + 65) & 63
            role = jnp.where(rel == 1, 0, jnp.where(rel == core_rel, 1, 2))
            slot = b * 6 + role * 2 + (n & 1)
            acc[slot] = acc[slot] + loc[b, j].astype(F32)
    for role, out in enumerate((d_own, x_core, x_edge)):
        for b in range(2):
            for h in range(2):
                out[128 * b : 128 * b + 128, 128 * h : 128 * h + 128] = acc[
                    b * 6 + role * 2 + h
                ].astype(BF16)
    copies[2].wait()
    copies[3].wait()
    for out in (x_core, x_edge):
        for i, v in enumerate(split3(obs[0]) + split3(obs[1])):
            out[256 + 16 * i : 272 + 16 * i, :] = v


def assemble_kernel(scal, e0, e1, e2, e3, out):
    for k, e in enumerate((e0, e1, e2, e3)):
        out[:, scal[1] ^ k] = e[...]


def band_apply(mats, x, exact):
    hi, lo = mats

    def mul(a, b):
        return jnp.dot(a, b, preferred_element_type=F32)

    if exact:
        return mul(hi, x) + mul(lo, x)
    xh = x.astype(BF16)
    xl = (x - xh.astype(F32)).astype(BF16)
    return mul(hi, xh) + (mul(lo, xh) + mul(hi, xl))


def smooth_rows(src, exact, mats, avb):
    for r in range(0, avb.shape[0], GRP):
        avb[r : r + GRP, :] = band_apply(mats, src(r), exact).astype(BF16)


def obs_rows(avb, umat, ens3, dmats, w, dxs, norm):
    lev = 32
    ms = avb.shape[0] // lev
    for i, (ens, d) in enumerate(zip(ens3, dmats)):
        umat[...] = lax.dot_general(
            avb[...], d, (((1,), (1,)), ((), ())), preferred_element_type=F32
        )

        def member(m, acc):
            e = ens[m].astype(F32).reshape(lev, 256)
            return acc + e * umat[pl.ds(pl.multiple_of(lev * m, lev), lev), :]

        dx = lax.fori_loop(0, ms, member, jnp.zeros((lev, 256), F32), unroll=4)
        dxs[:, 256 * i : 256 * i + 256] = dx * norm
    return jnp.dot(
        w[:, 0:lev], dxs[...], precision=lax.Precision.HIGHEST, preferred_element_type=F32
    )


def adjoint_rows(q, wt, ens3, dmats, ua, norm):
    lev = 32
    ms = ua.shape[0] // lev
    dxa = (
        jnp.dot(wt[:, 0:16], q, precision=lax.Precision.HIGHEST, preferred_element_type=F32)
        * norm
    )
    total = None
    for i, (ens, d) in enumerate(zip(ens3, dmats)):
        mine = dxa[:, 256 * i : 256 * i + 256]

        def member(m, _, ens=ens, mine=mine):
            e = ens[m].astype(F32).reshape(lev, 256)
            ua[pl.ds(pl.multiple_of(lev * m, lev), lev), :] = (e * mine).astype(BF16)
            return 0

        lax.fori_loop(0, ms, member, 0, unroll=4)
        part = jnp.dot(ua[...], d, preferred_element_type=F32)
        total = part if total is None else total + part
    return total


def adjoint_finish(mats, umat, out):
    ms = out.shape[0]
    lev = 32
    five = GRP // lev
    for i in range(0, ms, five):
        got = band_apply(mats, umat[lev * i : lev * i + GRP, :], False)
        out[i : i + five] = got.reshape(five, 4, 8, 256)


def obs_of(x):
    return (
        join3(x[256:272, :], x[272:288, :], x[288:304, :]),
        join3(x[304:320, :], x[320:336, :], x[336:352, :]),
    )


def first_kernel(
    norm, scal, c0, c1, c2, c3, e_own, e_core, d_own, x_core, bands,
    cm, avb, hx_core, hx_own, w, wt, src, wsq, umat, dxs,
):
    share = src.shape[0]
    wsq[...] = jnp.zeros(wsq.shape, F32)
    for k, c in enumerate((c0, c1, c2, c3)):
        group = scal[1] ^ k
        val = c[pl.ds(0, share)]
        cm[:, group] = val
        src[:, group] = val.astype(F32)
        wsq[pl.ds(pl.multiple_of(8 * group, 8), 8), :] = join3(
            c[share], c[share + 1], c[share + 2]
        )[:, 0:128]
    w[...] = wsq[...].T[0:16, :]
    wt[...] = wsq[0:32, :]

    def rows_of(r):
        five = GRP // 32
        return src[r // 32 : r // 32 + five].reshape(GRP, 256).astype(BF16)

    smooth_rows(rows_of, True, (bands[0], bands[1]), avb)
    hx = obs_rows(avb, umat, (e_own, e_core), (d_own[...], x_core[0:256, :]), w, dxs, norm)
    hx_own[...] = hx[:, 0:256]
    hx_core[...] = hx[:, 256:512]


def edge_kernel(norm, avb, e_edge, x_edge, w, hx_edge, umat, dxs):
    hx_edge[...] = obs_rows(avb, umat, (e_edge,), (x_edge[0:256, :],), w, dxs, norm)


def partial_kernel(norm, affine, h_oe, inv, inn, e_own, e_edge, d_own, x_edge, wt, out, ua):
    ie, ye = obs_of(x_edge)
    own, edge = h_oe[0:16, :], h_oe[16:32, :]
    if affine:
        own, edge = own - inn[...], edge - ye
    q = jnp.concatenate([inv[...] * own, ie * edge], axis=1)
    out[...] = adjoint_rows(
        q, wt, (e_own, e_edge), (d_own[...], x_edge[0:256, :]), ua, norm
    )


def second_kernel(
    norm, scal, part, h_core, cm, e_own, e_core, d_own, x_core, bands, w, wt, s0,
    a0, a1, a2, a3, avb, hx_core, hx_own, adj, ua, umat, dxs,
):
    share = adj.shape[0]
    ic, yc = obs_of(x_core)
    dcore = x_core[0:256, :]
    q = ic * (h_core[...] - yc)
    umat[...] = part[...] + adjoint_rows(q, wt, (e_core,), (dcore,), ua, norm)
    adjoint_finish((bands[2], bands[3]), umat, adj)
    for k, a in enumerate((a0, a1, a2, a3)):
        a[...] = adj[:, scal[1] ^ k].astype(BF16)

    def total(m, carry):
        gg, cg = carry
        c = cm[m].astype(F32)
        g = c + adj[m]
        adj[m] = g
        return gg + jnp.sum(g * g, axis=0), cg + jnp.sum(c * g, axis=0)

    zero = jnp.zeros((8, 256), F32)
    gg, cg = lax.fori_loop(0, share, total, (zero, zero), unroll=2)

    def rows_of(r):
        five = GRP // 32
        return adj[r // 32 : r // 32 + five].reshape(GRP, 256)

    smooth_rows(rows_of, False, (bands[0], bands[1]), avb)
    hx = obs_rows(avb, umat, (e_own, e_core), (d_own[...], dcore), w, dxs, norm)
    hx_own[...] = hx[:, 0:256]
    hx_core[0:16, :] = hx[:, 256:512]
    hx_core[16:24, :] = jnp.zeros((8, 256), F32)
    hx_core[16:17, :] = jnp.sum(s0[...], axis=0, keepdims=True)
    hx_core[17:18, :] = jnp.sum(gg, axis=0, keepdims=True)
    hx_core[18:19, :] = jnp.sum(cg, axis=0, keepdims=True)


def sums_kernel(hs, h_core, h1_oe, h1_core, inv, inn, x_core, out):
    ic, yc = obs_of(x_core)

    def rows(h1, i, y, d):
        diff = h1 - y
        q = i * diff
        return [
            jnp.sum(q * diff, axis=0, keepdims=True),
            jnp.sum(q * d, axis=0, keepdims=True),
            jnp.sum(i * d * d, axis=0, keepdims=True),
        ]

    own = rows(h1_oe[0:16, :], inv[...], inn[...], hs[0:16, :])
    core = rows(h1_core[...], ic, yc, h_core[...])
    out[...] = hs[32:40, :]
    for i in range(3):
        out[3 + i : 4 + i, :] = own[i] + core[i]


def third_kernel(
    norm, scal, part, h_core, e_core, x_core, bands, wt, a0, a1, a2, a3, adj, ua, umat
):
    ic, _ = obs_of(x_core)
    umat[...] = part[...] + adjoint_rows(
        ic * h_core[...], wt, (e_core,), (x_core[0:256, :],), ua, norm
    )
    adjoint_finish((bands[2], bands[3]), umat, adj)
    for k, a in enumerate((a0, a1, a2, a3)):
        a[...] = adj[:, scal[1] ^ k].astype(BF16)


def grad_first_kernel(scal, ctl, a0, a1, a2, a3, out, buf, sems):
    share = a0.shape[0]
    few = share // 4
    copies = []
    for k, a in enumerate((a0, a1, a2, a3)):
        for i in range(4):
            here = pl.ds(few * i, few)
            at = pl.ds(share * (scal[2] ^ k) + few * i, few)
            buf[k, here] = ctl[at] + a[here].astype(F32)
            copies.append(
                pltpu.make_async_copy(buf.at[k, here], out.at[at], sems.at[4 * k + i])
            )
            copies[-1].start()
    for c in copies:
        c.wait()


def grad_second_kernel(
    count, scal, ctl, a0, a1, a2, a3, b0, b1, b2, b3, sums, out, costs, buf, sems
):
    tot = jnp.sum(sums[...], axis=1, keepdims=True)
    cc, gg, cg = tot[0:1], tot[1:2], tot[2:3]
    dd, qd, rd = tot[3:4], tot[4:5], tot[5:6]
    tau = STEP / jnp.sqrt(gg / count + 1e-06)
    first = (0.5 * cc + 0.5 * dd) / count
    second = 0.5 * (cc - 2.0 * tau * cg + tau * tau * gg) + 0.5 * (
        dd - 2.0 * tau * qd + tau * tau * rd
    )
    tb = jnp.broadcast_to(tau, (8, 256))
    share = a0.shape[0]
    copies = []
    few = share // 4
    for k, (a, b) in enumerate(zip((a0, a1, a2, a3), (b0, b1, b2, b3))):
        for i in range(4):
            here = pl.ds(few * i, few)
            at = pl.ds(share * (scal[2] ^ k) + few * i, few)
            g = ctl[at] + a[here].astype(F32)
            buf[k, here] = g - tb * (g + b[here].astype(F32))
            copies.append(
                pltpu.make_async_copy(buf.at[k, here], out.at[at], sems.at[4 * k + i])
            )
            copies[-1].start()
    costs[0] = first[0, 0]
    costs[1] = (second / count)[0, 0]
    for c in copies:
        c.wait()


def make_pairs(tiles, levs):
    def flat(t, g):
        return t * levs + g

    def zh(t):
        return (t >> 3) & 1

    edge = []
    for t in range(tiles):
        e = (t + 1) % tiles if t & 1 else (t - 1) % tiles
        for g in range(levs):
            edge.append((flat(t, g), flat(e, g if zh(t) == zh(e) else g ^ 2)))
    far = [(flat(t, g), flat(t ^ 8, g ^ 2)) for t in range(tiles) for g in range(levs)]

    def tile_xor(k):
        return [(t, t ^ k) for t in range(tiles)]

    def lev_xor(k):
        return [(g, g ^ k) for g in range(levs)]

    return edge, far, tile_xor, lev_xor


def per_device(
    control, ensemble, loc_blocks, neighbours, vert_band, channel_weights, innovation, inv_error
):
    members, ldev, pdev = control.shape
    tiles = lax.axis_size("tile")
    levs = lax.axis_size("lev")
    lev = levs * ldev
    share = members // levs
    rows = share * lev
    norm = 1.0 / math.sqrt(members - 1)
    edge, far, tile_xor, lev_xor = make_pairs(tiles, levs)
    both = ("tile", "lev")
    tile_pos = lax.axis_index("tile").astype(jnp.int32)
    lev_pos = lax.axis_index("lev").astype(jnp.int32)
    mset = lev_pos ^ (2 * ((tile_pos >> 3) & 1))
    scal = jnp.stack([tile_pos, lev_pos, mset, mset])

    def swap_core(x):
        return lax.ppermute(x, "tile", tile_xor(1))

    def swap_edge(x):
        return lax.ppermute(x, both, edge)

    def shuffle(parts):
        return [parts[0]] + [
            lax.ppermute(parts[k], "lev", lev_xor(k)) for k in range(1, 4)
        ]

    def sum4(x, axis, pairs, steps):
        one, two, three = (
            lax.ppermute(x, axis, pairs(k)) for k in steps
        )
        return (x + one) + (two + three)

    chunk = sds((share, ldev, pdev), BF16)
    hbm = pl.BlockSpec(memory_space=pltpu.HBM)

    def far_off(x):
        return pltpu.with_memory_space_constraint(x, pltpu.HBM)

    eparts = call(
        pack_ens_kernel, [chunk] * 4, (scal, far_off(ensemble)), 1,
        [pltpu.SemaphoreType.DMA((4,))],
        specs=[SM, hbm],
    )
    eparts = shuffle(eparts)
    band = jnp.tile(vert_band.T, (1, 8))
    d_own, x_core, x_edge, bands = call(
        densify_kernel,
        [
            sds((256, 256), BF16), sds((352, 256), BF16), sds((352, 256), BF16),
            sds((4, GRP, GRP), BF16),
        ],
        (
            scal, neighbours, far_off(loc_blocks), far_off(inv_error), far_off(innovation), band,
        ),
        2,
        [
            pltpu.VMEM((12, 128, 128), F32), pltpu.VMEM(loc_blocks.shape, BF16),
            pltpu.VMEM((2,) + inv_error.shape, F32), pltpu.VMEM((256, 256), F32),
            pltpu.SemaphoreType.DMA((4,)),
        ],
        specs=[SM, SM, hbm, hbm, hbm, VM],
    )
    wt_own = jnp.pad(channel_weights.T, ((0, 0), (0, pdev - channel_weights.shape[0])))
    packed = call(
        pack_ctl_kernel,
        [sds((share + 3, ldev, pdev), BF16)] * 4 + [sds((ldev, pdev), F32)],
        (scal, control, wt_own),
        1,
    )
    s0 = packed[4]
    x_edge = swap_edge(x_edge)
    x_core = swap_core(x_core)
    field = sds((share, levs, ldev, pdev), BF16)
    (e_own,) = call(assemble_kernel, [field], (scal, *eparts), 1)
    e_edge = swap_edge(e_own)
    e_core = swap_core(e_own)
    cparts = shuffle(packed[:4])

    umat = pltpu.VMEM((rows, pdev), F32)
    half = pltpu.VMEM((rows, pdev), BF16)
    full = pltpu.VMEM((share, levs, ldev, pdev), F32)
    obs = channel_weights.shape[0]
    mm = 2 * rows * pdev * pdev
    row = sds((obs, pdev), F32)
    flat = sds((rows, pdev), BF16)
    wide = sds((rows, pdev), F32)

    def bind(fn, *given):
        def kernel(*refs):
            fn(*given, *refs)

        return kernel

    cm, avb, hx_core, hx_own, w, wt = call(
        bind(first_kernel, norm),
        [field, flat, row, row, sds((obs, 128), F32), sds((lev, 128), F32)],
        (scal, *cparts, e_own, e_core, d_own, x_core, bands),
        1,
        [full, pltpu.VMEM((128, 128), F32), umat, pltpu.VMEM((lev, 2 * pdev), F32)],
        3 * mm,
    )

    def reduce_obs(tag, core_msg, own, smooth):
        got = swap_core(core_msg)
        (edge_row,) = call(
            bind(edge_kernel, norm),
            [row],
            (smooth, e_edge, x_edge, w),
            0,
            [umat, pltpu.VMEM((lev, pdev), F32)],
            mm,
        )
        mine = jnp.concatenate([own + got[:obs], edge_row], axis=0)
        other = swap_edge(mine)
        tot = mine + jnp.concatenate([other[obs:], other[:obs]], axis=0)
        if core_msg.shape[0] > obs:
            extra = core_msg[obs:] + got[obs:]
            tot = jnp.concatenate([tot, extra], axis=0)
        tot = sum4(tot, "lev", lev_xor, (1, 2, 3))
        core = swap_core(tot[:obs])
        (part,) = call(
            bind(partial_kernel, norm, tag == "a"),
            [wide],
            (tot, inv_error, innovation, e_own, e_edge, d_own, x_edge, wt),
            0,
            [half],
            2 * mm,
        )
        return tot, core, part

    h1_oe, h1_core, part = reduce_obs("a", hx_core, hx_own, avb)
    outs = call(
        bind(second_kernel, norm),
        [chunk] * 4 + [flat, sds((obs + 8, pdev), F32), row],
        (scal, part, h1_core, cm, e_own, e_core, d_own, x_core, bands, w, wt, s0),
        1,
        [full, half, umat, pltpu.VMEM((lev, 2 * pdev), F32)],
        6 * mm,
    )
    aparts = shuffle(outs[:4])
    hs, hd_core, part = reduce_obs("b", outs[5], outs[6], outs[4])
    sums = call(
        sums_kernel,
        [sds((8, pdev), F32)],
        (hs, hd_core, h1_oe, h1_core, inv_error, innovation, x_core),
        0,
    )[0]
    bparts = call(
        bind(third_kernel, norm),
        [chunk] * 4,
        (scal, part, hd_core, e_core, x_core, bands, wt),
        1,
        [full, half, umat],
        3 * mm,
    )
    bparts = shuffle(bparts)
    sums = sums + lax.ppermute(sums, "tile", tile_xor(2))
    sums = sums + lax.ppermute(sums, "tile", tile_xor(6))
    sums = sums + lax.ppermute(sums, both, far)
    sums = sums + lax.ppermute(sums, "tile", tile_xor(16))
    sums = sums + lax.ppermute(sums, "tile", tile_xor(48))
    whole = sds((members, ldev, pdev), F32)
    anywhere = pl.BlockSpec(memory_space=pl.ANY)
    outbuf = [pltpu.VMEM((4, share, ldev, pdev), F32), pltpu.SemaphoreType.DMA((16,))]
    (grad_first,) = call(
        grad_first_kernel, [whole], (scal, control, *aparts), 1, outbuf,
        out_specs=(anywhere,),
    )
    count = float(members * lev * pdev * tiles)
    grad_second, costs = call(
        bind(grad_second_kernel, count),
        [whole, sds((2,), F32)],
        (scal, control, *aparts, *bparts, sums),
        1,
        outbuf,
        out_specs=(anywhere, SM),
    )
    return grad_first, grad_second, costs


def solution(mesh):
    placed = (
        P(None, "lev", "tile"),
        P(None, "lev", "tile"),
        P("tile", None, None, None),
        P("tile", None),
        P(),
        P(None, "lev"),
        P(None, "tile"),
        P(None, "tile"),
    )
    return jax.shard_map(
        per_device,
        mesh=mesh,
        in_specs=placed,
        out_specs=(P(None, "lev", "tile"), P(None, "lev", "tile"), P()),
        check_vma=False,
    )
```

```python
import math

import jax
import jax.numpy as jnp
from jax import lax
from jax.experimental import pallas as pl
from jax.experimental.pallas import tpu as pltpu
from jax.sharding import PartitionSpec as P


HV = 4
NS = 2 * HV + 1
STEP = 0.5
GRP = 160
F32 = jnp.float32
BF16 = jnp.bfloat16
VM = pl.BlockSpec(memory_space=pltpu.VMEM)
SM = pl.BlockSpec(memory_space=pltpu.SMEM)


def call(body, outs, args, scalars, scratch=(), flops=0, specs=None, out_specs=None):
    if specs is None:
        specs = [SM] * scalars + [VM] * (len(args) - scalars)
    if out_specs is None:
        out_specs = tuple(VM for _ in outs)
    moved = sum(a.size * a.dtype.itemsize for a in args)
    moved += sum(math.prod(o.shape) * jnp.dtype(o.dtype).itemsize for o in outs)
    return pl.pallas_call(
        body,
        out_shape=tuple(outs),
        in_specs=specs,
        out_specs=out_specs,
        scratch_shapes=list(scratch),
        cost_estimate=pl.CostEstimate(flops=flops, bytes_accessed=moved, transcendentals=0),
        compiler_params=pltpu.CompilerParams(vmem_limit_bytes=48 * 1024 * 1024),
    )(*args)


def sds(shape, dtype):
    return jax.ShapeDtypeStruct(shape, dtype)


def split3(x):
    hi = x.astype(BF16)
    rest = x - hi.astype(F32)
    mid = rest.astype(BF16)
    lo = (rest - mid.astype(F32)).astype(BF16)
    return hi, mid, lo


def join3(hi, mid, lo):
    return (hi.astype(F32) + mid.astype(F32)) + lo.astype(F32)


def pack_ens_kernel(scal, ens, *refs):
    outs, sems = refs[:4], refs[4]
    share = outs[0].shape[0]
    copies = [
        pltpu.make_async_copy(
            ens.at[pl.ds(share * (scal[2] ^ k), share)], outs[k], sems.at[k]
        )
        for k in range(4)
    ]
    for c in copies:
        c.start()
    for c in copies:
        c.wait()


def pack_ctl_kernel(scal, ctl, wt, *outs):
    share = outs[0].shape[0] - 3
    parts = split3(wt[...])
    for k in range(4):
        outs[k][pl.ds(0, share)] = ctl[pl.ds(share * (scal[2] ^ k), share)].astype(BF16)
        for i in range(3):
            outs[k][share + i] = parts[i]
    sq = jnp.zeros(outs[4].shape, F32)

    def body(m, acc):
        v = ctl[m]
        return acc + v * v

    outs[4][...] = lax.fori_loop(0, ctl.shape[0], body, sq, unroll=4)


def densify_kernel(
    scal, nb_hbm, loc_hbm, inv_hbm, inn_hbm, vbt_hbm, d_own, x_core, x_edge, bands, obs, acc, loc, mat,
    narrow, nb, vbt, sems,
):
    copies = [
        pltpu.make_async_copy(loc_hbm.at[0], loc.at[0], sems.at[0]),
        pltpu.make_async_copy(loc_hbm.at[1], loc.at[1], sems.at[1]),
        pltpu.make_async_copy(inv_hbm, obs.at[0], sems.at[2]),
        pltpu.make_async_copy(inn_hbm, obs.at[1], sems.at[3]),
        pltpu.make_async_copy(nb_hbm, nb, sems.at[4]),
        pltpu.make_async_copy(vbt_hbm, vbt, sems.at[5]),
    ]
    for c in copies:
        c.start()
    narrow[...] = jnp.zeros(narrow.shape, F32)
    copies[5].wait()
    narrow[0:NS, 0:32] = vbt[...]
    band = narrow[...]
    band = band + pltpu.roll(band, 32, 1)
    band = band + pltpu.roll(band, 64, 1)
    band = jnp.concatenate([band, band], axis=1)
    row = lax.broadcasted_iota(jnp.int32, (256, 256), 0)
    col = lax.broadcasted_iota(jnp.int32, (256, 256), 1)
    shift = row - col
    same = (row >> 5) == (col >> 5)
    tot = jnp.zeros((256, 256), F32)
    for s in range(NS):
        tot = jnp.where(same & (shift == s - HV), band[s : s + 1, :], tot)
    mat[...] = tot
    back = mat[...]
    fwd = mat[...].T
    for i, m in enumerate((fwd, back)):
        hi = m.astype(BF16)
        bands[2 * i] = hi[0:GRP, 0:GRP]
        bands[2 * i + 1] = (m - hi.astype(F32)).astype(BF16)[0:GRP, 0:GRP]
    tile = scal[0]
    core_rel = 2 - 2 * (tile & 1)
    acc[...] = jnp.zeros(acc.shape, F32)
    copies[4].wait()
    for b in range(2):
        copies[b].wait()
        for j in range(loc.shape[1]):
            n = nb[b, j]
            rel = ((n >> 1) - tile + 65) & 63
            role = jnp.where(rel == 1, 0, jnp.where(rel == core_rel, 1, 2))
            slot = b * 6 + role * 2 + (n & 1)
            acc[slot] = acc[slot] + loc[b, j].astype(F32)
    for role, out in enumerate((d_own, x_core, x_edge)):
        for b in range(2):
            for h in range(2):
                out[128 * b : 128 * b + 128, 128 * h : 128 * h + 128] = acc[
                    b * 6 + role * 2 + h
                ].astype(BF16)
    copies[2].wait()
    copies[3].wait()
    for out in (x_core, x_edge):
        for i, v in enumerate(split3(obs[0]) + split3(obs[1])):
            out[256 + 16 * i : 272 + 16 * i, :] = v


def assemble_kernel(scal, e0, e1, e2, e3, out):
    for k, e in enumerate((e0, e1, e2, e3)):
        out[:, scal[1] ^ k] = e[...]


def band_apply(mats, x, exact):
    hi, lo = mats

    def mul(a, b):
        return jnp.dot(a, b, preferred_element_type=F32)

    if exact:
        return mul(hi, x) + mul(lo, x)
    xh = x.astype(BF16)
    xl = (x - xh.astype(F32)).astype(BF16)
    return mul(hi, xh) + (mul(lo, xh) + mul(hi, xl))


def smooth_rows(src, exact, mats, avb):
    for r in range(0, avb.shape[0], GRP):
        avb[r : r + GRP, :] = band_apply(mats, src(r), exact).astype(BF16)


def obs_rows(avb, umat, ens3, dmats, w, dxs, norm):
    lev = 32
    ms = avb.shape[0] // lev
    for i, (ens, d) in enumerate(zip(ens3, dmats)):
        umat[...] = lax.dot_general(
            avb[...], d, (((1,), (1,)), ((), ())), preferred_element_type=F32
        )

        def member(m, acc):
            e = ens[m].astype(F32).reshape(lev, 256)
            return acc + e * umat[pl.ds(pl.multiple_of(lev * m, lev), lev), :]

        dx = lax.fori_loop(0, ms, member, jnp.zeros((lev, 256), F32), unroll=4)
        dxs[:, 256 * i : 256 * i + 256] = dx * norm
    return jnp.dot(
        w[:, 0:lev], dxs[...], precision=lax.Precision.HIGHEST, preferred_element_type=F32
    )


def adjoint_rows(q, wt, ens3, dmats, ua, norm):
    lev = 32
    ms = ua.shape[0] // lev
    dxa = (
        jnp.dot(wt[:, 0:16], q, precision=lax.Precision.HIGHEST, preferred_element_type=F32)
        * norm
    )
    total = None
    for i, (ens, d) in enumerate(zip(ens3, dmats)):
        mine = dxa[:, 256 * i : 256 * i + 256]

        def member(m, _, ens=ens, mine=mine):
            e = ens[m].astype(F32).reshape(lev, 256)
            ua[pl.ds(pl.multiple_of(lev * m, lev), lev), :] = (e * mine).astype(BF16)
            return 0

        lax.fori_loop(0, ms, member, 0, unroll=4)
        part = jnp.dot(ua[...], d, preferred_element_type=F32)
        total = part if total is None else total + part
    return total


def adjoint_finish(mats, umat, out):
    ms = out.shape[0]
    lev = 32
    five = GRP // lev
    for i in range(0, ms, five):
        got = band_apply(mats, umat[lev * i : lev * i + GRP, :], False)
        out[i : i + five] = got.reshape(five, 4, 8, 256)


def obs_of(x):
    return (
        join3(x[256:272, :], x[272:288, :], x[288:304, :]),
        join3(x[304:320, :], x[320:336, :], x[336:352, :]),
    )


def first_kernel(
    norm, scal, c0, c1, c2, c3, e_own, e_core, d_own, x_core, bands,
    cm, avb, hx_core, hx_own, w, wt, src, wsq, umat, dxs,
):
    share = src.shape[0]
    wsq[...] = jnp.zeros(wsq.shape, F32)
    for k, c in enumerate((c0, c1, c2, c3)):
        group = scal[1] ^ k
        val = c[pl.ds(0, share)]
        cm[:, group] = val
        src[:, group] = val.astype(F32)
        wsq[pl.ds(pl.multiple_of(8 * group, 8), 8), :] = join3(
            c[share], c[share + 1], c[share + 2]
        )[:, 0:128]
    w[...] = wsq[...].T[0:16, :]
    wt[...] = wsq[0:32, :]

    def rows_of(r):
        five = GRP // 32
        return src[r // 32 : r // 32 + five].reshape(GRP, 256).astype(BF16)

    smooth_rows(rows_of, True, (bands[0], bands[1]), avb)
    hx = obs_rows(avb, umat, (e_own, e_core), (d_own[...], x_core[0:256, :]), w, dxs, norm)
    hx_own[...] = hx[:, 0:256]
    hx_core[...] = hx[:, 256:512]


def edge_kernel(norm, avb, e_edge, x_edge, w, hx_edge, umat, dxs):
    hx_edge[...] = obs_rows(avb, umat, (e_edge,), (x_edge[0:256, :],), w, dxs, norm)


def partial_kernel(norm, affine, h_oe, obs, e_own, e_edge, d_own, x_edge, wt, out, ua):
    ie, ye = obs_of(x_edge)
    own, edge = h_oe[0:16, :], h_oe[16:32, :]
    if affine:
        own, edge = own - obs[1], edge - ye
    q = jnp.concatenate([obs[0] * own, ie * edge], axis=1)
    out[...] = adjoint_rows(
        q, wt, (e_own, e_edge), (d_own[...], x_edge[0:256, :]), ua, norm
    )


def second_kernel(
    norm, scal, part, h_core, cm, e_own, e_core, d_own, x_core, bands, w, wt, s0,
    a0, a1, a2, a3, avb, hx_core, hx_own, adj, ua, umat, dxs,
):
    share = adj.shape[0]
    ic, yc = obs_of(x_core)
    dcore = x_core[0:256, :]
    q = ic * (h_core[...] - yc)
    umat[...] = part[...] + adjoint_rows(q, wt, (e_core,), (dcore,), ua, norm)
    adjoint_finish((bands[2], bands[3]), umat, adj)
    for k, a in enumerate((a0, a1, a2, a3)):
        a[...] = adj[:, scal[1] ^ k].astype(BF16)

    def total(m, carry):
        gg, cg = carry
        c = cm[m].astype(F32)
        g = c + adj[m]
        adj[m] = g
        return gg + jnp.sum(g * g, axis=0), cg + jnp.sum(c * g, axis=0)

    zero = jnp.zeros((8, 256), F32)
    gg, cg = lax.fori_loop(0, share, total, (zero, zero), unroll=2)

    def rows_of(r):
        five = GRP // 32
        return adj[r // 32 : r // 32 + five].reshape(GRP, 256)

    smooth_rows(rows_of, False, (bands[0], bands[1]), avb)
    hx = obs_rows(avb, umat, (e_own, e_core), (d_own[...], dcore), w, dxs, norm)
    hx_own[...] = hx[:, 0:256]
    hx_core[0:16, :] = hx[:, 256:512]
    hx_core[16:24, :] = jnp.zeros((8, 256), F32)
    hx_core[16:17, :] = jnp.sum(s0[...], axis=0, keepdims=True)
    hx_core[17:18, :] = jnp.sum(gg, axis=0, keepdims=True)
    hx_core[18:19, :] = jnp.sum(cg, axis=0, keepdims=True)


def misfit_kernel(h1_oe, h1_core, obs, x_core, out):
    ic, yc = obs_of(x_core)
    own = h1_oe[0:16, :] - obs[1]
    core = h1_core[...] - yc
    qo = obs[0] * own
    qc = ic * core
    out[0:16, :] = qo
    out[16:32, :] = qc
    out[32:40, :] = jnp.zeros((8, 256), F32)
    out[32:33, :] = jnp.sum(qo * own, axis=0, keepdims=True) + jnp.sum(
        qc * core, axis=0, keepdims=True
    )


def sums_kernel(hs, h_core, misfit, obs, x_core, out):
    ic, _ = obs_of(x_core)
    do, dc = hs[0:16, :], h_core[...]

    def both(own, core):
        return jnp.sum(own, axis=0, keepdims=True) + jnp.sum(core, axis=0, keepdims=True)

    out[...] = hs[32:40, :]
    out[3:4, :] = misfit[32:33, :]
    out[4:5, :] = both(misfit[0:16, :] * do, misfit[16:32, :] * dc)
    out[5:6, :] = both(obs[0] * do * do, ic * dc * dc)


def third_kernel(
    norm, scal, part, h_core, e_core, x_core, bands, wt, a0, a1, a2, a3, adj, ua, umat
):
    ic, _ = obs_of(x_core)
    umat[...] = part[...] + adjoint_rows(
        ic * h_core[...], wt, (e_core,), (x_core[0:256, :],), ua, norm
    )
    adjoint_finish((bands[2], bands[3]), umat, adj)
    for k, a in enumerate((a0, a1, a2, a3)):
        a[...] = adj[:, scal[1] ^ k].astype(BF16)


def grad_first_kernel(scal, ctl, a0, a1, a2, a3, out):
    share = a0.shape[0]
    for k, a in enumerate((a0, a1, a2, a3)):
        at = pl.ds(share * (scal[2] ^ k), share)
        out[at] = ctl[at] + a[...].astype(F32)


def grad_second_kernel(
    count, scal, ctl, a0, a1, a2, a3, b0, b1, b2, b3, sums, out, costs
):
    tot = jnp.sum(sums[...], axis=1, keepdims=True)
    cc, gg, cg = tot[0:1], tot[1:2], tot[2:3]
    dd, qd, rd = tot[3:4], tot[4:5], tot[5:6]
    tau = STEP / jnp.sqrt(gg / count + 1e-06)
    first = (0.5 * cc + 0.5 * dd) / count
    second = 0.5 * (cc - 2.0 * tau * cg + tau * tau * gg) + 0.5 * (
        dd - 2.0 * tau * qd + tau * tau * rd
    )
    tb = jnp.broadcast_to(tau, (8, 256))
    share = a0.shape[0]
    for k, (a, b) in enumerate(zip((a0, a1, a2, a3), (b0, b1, b2, b3))):
        base = share * (scal[2] ^ k)

        def body(m, _, a=a, b=b, base=base):
            g = ctl[base + m] + a[m].astype(F32)
            out[base + m] = g - tb * (g + b[m].astype(F32))
            return 0

        lax.fori_loop(0, share, body, 0, unroll=10)
    costs[0] = first[0, 0]
    costs[1] = (second / count)[0, 0]


def make_pairs(tiles, levs):
    def flat(t, g):
        return t * levs + g

    def zh(t):
        return (t >> 3) & 1

    edge = []
    for t in range(tiles):
        e = (t + 1) % tiles if t & 1 else (t - 1) % tiles
        for g in range(levs):
            edge.append((flat(t, g), flat(e, g if zh(t) == zh(e) else g ^ 2)))
    far = [(flat(t, g), flat(t ^ 8, g ^ 2)) for t in range(tiles) for g in range(levs)]

    def tile_xor(k):
        return [(t, t ^ k) for t in range(tiles)]

    def lev_xor(k):
        return [(g, g ^ k) for g in range(levs)]

    return edge, far, tile_xor, lev_xor


def per_device(
    control, ensemble, loc_blocks, neighbours, vert_band, channel_weights, innovation, inv_error
):
    members, ldev, pdev = control.shape
    tiles = lax.axis_size("tile")
    levs = lax.axis_size("lev")
    lev = levs * ldev
    share = members // levs
    rows = share * lev
    norm = 1.0 / math.sqrt(members - 1)
    edge, far, tile_xor, lev_xor = make_pairs(tiles, levs)
    both = ("tile", "lev")
    tile_pos = lax.axis_index("tile").astype(jnp.int32)
    lev_pos = lax.axis_index("lev").astype(jnp.int32)
    mset = lev_pos ^ (2 * ((tile_pos >> 3) & 1))
    scal = jnp.stack([tile_pos, lev_pos, mset, mset])

    def swap_core(x):
        return lax.ppermute(x, "tile", tile_xor(1))

    def swap_edge(x):
        return lax.ppermute(x, both, edge)

    def shuffle(parts):
        return [parts[0]] + [
            lax.ppermute(parts[k], "lev", lev_xor(k)) for k in range(1, 4)
        ]

    def sum4(x, axis, pairs, steps):
        one, two, three = (
            lax.ppermute(x, axis, pairs(k)) for k in steps
        )
        return (x + one) + (two + three)

    chunk = sds((share, ldev, pdev), BF16)
    hbm = pl.BlockSpec(memory_space=pltpu.HBM)

    def far_off(x):
        return pltpu.with_memory_space_constraint(x, pltpu.HBM)

    eparts = call(
        pack_ens_kernel, [chunk] * 4, (scal, far_off(ensemble)), 1,
        [pltpu.SemaphoreType.DMA((4,))],
        specs=[SM, hbm],
    )
    eparts = shuffle(eparts)
    obs_n = channel_weights.shape[0]
    d_own, x_core, x_edge, bands, obs_own = call(
        densify_kernel,
        [
            sds((256, 256), BF16), sds((352, 256), BF16), sds((352, 256), BF16),
            sds((4, GRP, GRP), BF16), sds((2, obs_n, pdev), F32),
        ],
        (
            scal, far_off(neighbours), far_off(loc_blocks), far_off(inv_error),
            far_off(innovation), far_off(vert_band.T),
        ),
        1,
        [
            pltpu.VMEM((12, 128, 128), F32), pltpu.VMEM(loc_blocks.shape, BF16),
            pltpu.VMEM((256, 256), F32), pltpu.VMEM((16, 128), F32),
            pltpu.SMEM(neighbours.shape, jnp.int32), pltpu.VMEM((NS, lev), F32),
            pltpu.SemaphoreType.DMA((6,)),
        ],
        specs=[SM, hbm, hbm, hbm, hbm, hbm],
    )
    wt_own = jnp.pad(channel_weights.T, ((0, 0), (0, pdev - channel_weights.shape[0])))
    packed = call(
        pack_ctl_kernel,
        [sds((share + 3, ldev, pdev), BF16)] * 4 + [sds((ldev, pdev), F32)],
        (scal, control, wt_own),
        1,
    )
    s0 = packed[4]
    x_edge = swap_edge(x_edge)
    x_core = swap_core(x_core)
    field = sds((share, levs, ldev, pdev), BF16)
    (e_own,) = call(assemble_kernel, [field], (scal, *eparts), 1)
    e_edge = swap_edge(e_own)
    e_core = swap_core(e_own)
    cparts = shuffle(packed[:4])

    umat = pltpu.VMEM((rows, pdev), F32)
    half = pltpu.VMEM((rows, pdev), BF16)
    full = pltpu.VMEM((share, levs, ldev, pdev), F32)
    obs = channel_weights.shape[0]
    mm = 2 * rows * pdev * pdev
    row = sds((obs, pdev), F32)
    flat = sds((rows, pdev), BF16)
    wide = sds((rows, pdev), F32)

    def bind(fn, *given):
        def kernel(*refs):
            fn(*given, *refs)

        return kernel

    cm, avb, hx_core, hx_own, w, wt = call(
        bind(first_kernel, norm),
        [field, flat, row, row, sds((obs, 128), F32), sds((lev, 128), F32)],
        (scal, *cparts, e_own, e_core, d_own, x_core, bands),
        1,
        [full, pltpu.VMEM((128, 128), F32), umat, pltpu.VMEM((lev, 2 * pdev), F32)],
        3 * mm,
    )

    def reduce_obs(tag, core_msg, own, smooth):
        got = swap_core(core_msg)
        (edge_row,) = call(
            bind(edge_kernel, norm),
            [row],
            (smooth, e_edge, x_edge, w),
            0,
            [umat, pltpu.VMEM((lev, pdev), F32)],
            mm,
        )
        mine = jnp.concatenate([own + got[:obs], edge_row], axis=0)
        other = swap_edge(mine)
        tot = mine + jnp.concatenate([other[obs:], other[:obs]], axis=0)
        if core_msg.shape[0] > obs:
            extra = core_msg[obs:] + got[obs:]
            tot = jnp.concatenate([tot, extra], axis=0)
        tot = sum4(tot, "lev", lev_xor, (1, 2, 3))
        core = swap_core(tot[:obs])
        (part,) = call(
            bind(partial_kernel, norm, tag == "a"),
            [wide],
            (tot, obs_own, e_own, e_edge, d_own, x_edge, wt),
            0,
            [half],
            2 * mm,
        )
        return tot, core, part

    h1_oe, h1_core, part = reduce_obs("a", hx_core, hx_own, avb)
    outs = call(
        bind(second_kernel, norm),
        [chunk] * 4 + [flat, sds((obs + 8, pdev), F32), row],
        (scal, part, h1_core, cm, e_own, e_core, d_own, x_core, bands, w, wt, s0),
        1,
        [full, half, umat, pltpu.VMEM((lev, 2 * pdev), F32)],
        6 * mm,
    )
    aparts = shuffle(outs[:4])
    (misfit,) = call(
        misfit_kernel, [sds((40, pdev), F32)], (h1_oe, h1_core, obs_own, x_core), 0
    )
    hs, hd_core, part = reduce_obs("b", outs[5], outs[6], outs[4])
    sums = call(
        sums_kernel, [sds((8, pdev), F32)], (hs, hd_core, misfit, obs_own, x_core), 0
    )[0]
    bparts = call(
        bind(third_kernel, norm),
        [chunk] * 4,
        (scal, part, hd_core, e_core, x_core, bands, wt),
        1,
        [full, half, umat],
        3 * mm,
    )
    bparts = shuffle(bparts)
    sums = sums + lax.ppermute(sums, "tile", tile_xor(2))
    sums = sums + lax.ppermute(sums, "tile", tile_xor(6))
    sums = sums + lax.ppermute(sums, both, far)
    sums = sums + lax.ppermute(sums, "tile", tile_xor(16))
    sums = sums + lax.ppermute(sums, "tile", tile_xor(48))
    whole = sds((members, ldev, pdev), F32)
    (grad_first,) = call(grad_first_kernel, [whole], (scal, control, *aparts), 1)
    count = float(members * lev * pdev * tiles)
    grad_second, costs = call(
        bind(grad_second_kernel, count),
        [whole, sds((2,), F32)],
        (scal, control, *aparts, *bparts, sums),
        1,
        out_specs=(VM, SM),
    )
    return grad_first, grad_second, costs


def solution(mesh):
    placed = (
        P(None, "lev", "tile"),
        P(None, "lev", "tile"),
        P("tile", None, None, None),
        P("tile", None),
        P(),
        P(None, "lev"),
        P(None, "tile"),
        P(None, "tile"),
    )
    return jax.shard_map(
        per_device,
        mesh=mesh,
        in_specs=placed,
        out_specs=(P(None, "lev", "tile"), P(None, "lev", "tile"), P()),
        check_vma=False,
    )
```

```python
import math

import jax
import jax.numpy as jnp
from jax import lax
from jax.experimental import pallas as pl
from jax.experimental.pallas import tpu as pltpu
from jax.sharding import PartitionSpec as P


HV = 4
NS = 2 * HV + 1
STEP = 0.5
GRP = 128
F32 = jnp.float32
BF16 = jnp.bfloat16
VM = pl.BlockSpec(memory_space=pltpu.VMEM)
SM = pl.BlockSpec(memory_space=pltpu.SMEM)


def call(body, outs, args, scalars, scratch=(), flops=0, specs=None, out_specs=None):
    if specs is None:
        specs = [SM] * scalars + [VM] * (len(args) - scalars)
    if out_specs is None:
        out_specs = tuple(VM for _ in outs)
    moved = sum(a.size * a.dtype.itemsize for a in args)
    moved += sum(math.prod(o.shape) * jnp.dtype(o.dtype).itemsize for o in outs)
    return pl.pallas_call(
        body,
        out_shape=tuple(outs),
        in_specs=specs,
        out_specs=out_specs,
        scratch_shapes=list(scratch),
        cost_estimate=pl.CostEstimate(flops=flops, bytes_accessed=moved, transcendentals=0),
        compiler_params=pltpu.CompilerParams(vmem_limit_bytes=48 * 1024 * 1024),
    )(*args)


def sds(shape, dtype):
    return jax.ShapeDtypeStruct(shape, dtype)


def split3(x):
    hi = x.astype(BF16)
    rest = x - hi.astype(F32)
    mid = rest.astype(BF16)
    lo = (rest - mid.astype(F32)).astype(BF16)
    return hi, mid, lo


def join3(hi, mid, lo):
    return (hi.astype(F32) + mid.astype(F32)) + lo.astype(F32)


def pack_ens_kernel(scal, ens, *refs):
    outs, sems = refs[:4], refs[4]
    share = outs[0].shape[0]
    copies = [
        pltpu.make_async_copy(
            ens.at[pl.ds(share * (scal[2] ^ k), share)], outs[k], sems.at[k]
        )
        for k in range(4)
    ]
    for c in copies:
        c.start()
    for c in copies:
        c.wait()


def pack_ctl_kernel(scal, ctl, wt, *outs):
    share = outs[0].shape[0] - 3
    parts = split3(wt[...])
    for k in range(4):
        outs[k][pl.ds(0, share)] = ctl[pl.ds(share * (scal[2] ^ k), share)].astype(BF16)
        for i in range(3):
            outs[k][share + i] = parts[i]
    sq = jnp.zeros(outs[4].shape, F32)

    def body(m, acc):
        v = ctl[m]
        return acc + v * v

    outs[4][...] = lax.fori_loop(0, ctl.shape[0], body, sq, unroll=4)


def densify_kernel(
    scal, nb_hbm, loc_hbm, inv_hbm, inn_hbm, vbt_hbm, d_own, x_core, x_edge, bands, obs, acc, loc, mat,
    narrow, nb, vbt, sems,
):
    copies = [
        pltpu.make_async_copy(loc_hbm.at[0], loc.at[0], sems.at[0]),
        pltpu.make_async_copy(loc_hbm.at[1], loc.at[1], sems.at[1]),
        pltpu.make_async_copy(inv_hbm, obs.at[0], sems.at[2]),
        pltpu.make_async_copy(inn_hbm, obs.at[1], sems.at[3]),
        pltpu.make_async_copy(nb_hbm, nb, sems.at[4]),
        pltpu.make_async_copy(vbt_hbm, vbt, sems.at[5]),
    ]
    for c in copies:
        c.start()
    narrow[...] = jnp.zeros(narrow.shape, F32)
    copies[5].wait()
    narrow[0:NS, 0:32] = vbt[...]
    band = narrow[...]
    band = band + pltpu.roll(band, 32, 1)
    band = band + pltpu.roll(band, 64, 1)
    row = lax.broadcasted_iota(jnp.int32, (GRP, GRP), 0)
    col = lax.broadcasted_iota(jnp.int32, (GRP, GRP), 1)
    shift = row - col
    same = (row >> 5) == (col >> 5)
    tot = jnp.zeros((GRP, GRP), F32)
    for s in range(NS):
        tot = jnp.where(same & (shift == s - HV), band[s : s + 1, :], tot)
    mat[...] = tot
    back = mat[...]
    fwd = mat[...].T
    for i, m in enumerate((fwd, back)):
        hi = m.astype(BF16)
        bands[i, :, 0:GRP] = hi
        bands[i, :, GRP : 2 * GRP] = hi
        bands[i, :, 2 * GRP : 3 * GRP] = (m - hi.astype(F32)).astype(BF16)
    tile = scal[0]
    core_rel = 2 - 2 * (tile & 1)
    acc[...] = jnp.zeros(acc.shape, F32)
    copies[4].wait()
    for b in range(2):
        copies[b].wait()
        for j in range(loc.shape[1]):
            n = nb[b, j]
            rel = ((n >> 1) - tile + 65) & 63
            role = jnp.where(rel == 1, 0, jnp.where(rel == core_rel, 1, 2))
            slot = b * 6 + role * 2 + (n & 1)
            acc[slot] = acc[slot] + loc[b, j].astype(F32)
    for role, out in enumerate((d_own, x_core, x_edge)):
        for b in range(2):
            for h in range(2):
                out[128 * b : 128 * b + 128, 128 * h : 128 * h + 128] = acc[
                    b * 6 + role * 2 + h
                ].astype(BF16)
    copies[2].wait()
    copies[3].wait()
    for out in (x_core, x_edge):
        for i, v in enumerate(split3(obs[0]) + split3(obs[1])):
            out[256 + 16 * i : 272 + 16 * i, :] = v


def assemble_kernel(scal, e0, e1, e2, e3, out):
    for k, e in enumerate((e0, e1, e2, e3)):
        out[:, scal[1] ^ k] = e[...]


def band_apply(mat, x, exact):
    if exact:
        return jnp.dot(
            mat[:, GRP : 3 * GRP], jnp.concatenate([x, x], axis=0), preferred_element_type=F32
        )
    xh = x.astype(BF16)
    xl = (x - xh.astype(F32)).astype(BF16)
    return jnp.dot(mat, jnp.concatenate([xh, xl, xh], axis=0), preferred_element_type=F32)


def smooth_rows(src, exact, mat, avb):
    for r in range(0, avb.shape[0], GRP):
        avb[r : r + GRP, :] = band_apply(mat, src(r), exact).astype(BF16)


def obs_rows(avb, umat, ens3, dmats, w, dxs, norm):
    lev = 32
    ms = avb.shape[0] // lev
    for i, (ens, d) in enumerate(zip(ens3, dmats)):
        umat[...] = lax.dot_general(
            avb[...], d, (((1,), (1,)), ((), ())), preferred_element_type=F32
        )

        def member(m, acc):
            e = ens[m].astype(F32).reshape(lev, 256)
            return acc + e * umat[pl.ds(pl.multiple_of(lev * m, lev), lev), :]

        dx = lax.fori_loop(0, ms, member, jnp.zeros((lev, 256), F32), unroll=4)
        dxs[:, 256 * i : 256 * i + 256] = dx * norm
    return jnp.dot(
        w[:, 0:lev], dxs[...], precision=lax.Precision.HIGHEST, preferred_element_type=F32
    )


def adjoint_rows(q, wt, ens3, dmats, ua, norm):
    lev = 32
    ms = ua.shape[0] // lev
    dxa = (
        jnp.dot(wt[:, 0:16], q, precision=lax.Precision.HIGHEST, preferred_element_type=F32)
        * norm
    )
    total = None
    for i, (ens, d) in enumerate(zip(ens3, dmats)):
        mine = dxa[:, 256 * i : 256 * i + 256]

        def member(m, _, ens=ens, mine=mine):
            e = ens[m].astype(F32).reshape(lev, 256)
            ua[pl.ds(pl.multiple_of(lev * m, lev), lev), :] = (e * mine).astype(BF16)
            return 0

        lax.fori_loop(0, ms, member, 0, unroll=4)
        part = jnp.dot(ua[...], d, preferred_element_type=F32)
        total = part if total is None else total + part
    return total


def adjoint_finish(mat, umat, out):
    lev = 32
    some = GRP // lev
    for i in range(0, out.shape[0], some):
        got = band_apply(mat, umat[lev * i : lev * i + GRP, :], False)
        out[i : i + some] = got.reshape(some, 4, 8, 256)


def obs_of(x):
    return (
        join3(x[256:272, :], x[272:288, :], x[288:304, :]),
        join3(x[304:320, :], x[320:336, :], x[336:352, :]),
    )


def first_kernel(
    norm, scal, c0, c1, c2, c3, e_own, e_core, d_own, x_core, bands,
    cm, avb, hx_core, hx_own, w, wt, src, wsq, umat, dxs,
):
    share = src.shape[0]
    wsq[...] = jnp.zeros(wsq.shape, F32)
    for k, c in enumerate((c0, c1, c2, c3)):
        group = scal[1] ^ k
        val = c[pl.ds(0, share)]
        cm[:, group] = val
        src[:, group] = val.astype(F32)
        wsq[pl.ds(pl.multiple_of(8 * group, 8), 8), :] = join3(
            c[share], c[share + 1], c[share + 2]
        )[:, 0:128]
    w[...] = wsq[...].T[0:16, :]
    wt[...] = wsq[0:32, :]

    def rows_of(r):
        some = GRP // 32
        return src[r // 32 : r // 32 + some].reshape(GRP, 256).astype(BF16)

    smooth_rows(rows_of, True, bands[0], avb)
    hx = obs_rows(avb, umat, (e_own, e_core), (d_own[...], x_core[0:256, :]), w, dxs, norm)
    hx_own[...] = hx[:, 0:256]
    hx_core[...] = hx[:, 256:512]


def edge_kernel(norm, avb, e_edge, x_edge, w, hx_edge, umat, dxs):
    hx_edge[...] = obs_rows(avb, umat, (e_edge,), (x_edge[0:256, :],), w, dxs, norm)


def own_edge_kernel(norm, avb, e_own, e_edge, d_own, x_edge, w, hx_own, hx_edge, umat, dxs):
    hx = obs_rows(
        avb, umat, (e_own, e_edge), (d_own[...], x_edge[0:256, :]), w, dxs, norm
    )
    hx_own[...] = hx[:, 0:256]
    hx_edge[...] = hx[:, 256:512]


def partial_kernel(norm, affine, h_oe, obs, e_own, e_edge, d_own, x_edge, wt, out, ua):
    ie, ye = obs_of(x_edge)
    own, edge = h_oe[0:16, :], h_oe[16:32, :]
    if affine:
        own, edge = own - obs[1], edge - ye
    q = jnp.concatenate([obs[0] * own, ie * edge], axis=1)
    out[...] = adjoint_rows(
        q, wt, (e_own, e_edge), (d_own[...], x_edge[0:256, :]), ua, norm
    )


def second_kernel(
    norm, scal, part, h_core, cm, e_core, x_core, bands, w, wt, s0,
    a0, a1, a2, a3, avb, hx_core, adj, ua, umat, dxs,
):
    share = adj.shape[0]
    ic, yc = obs_of(x_core)
    dcore = x_core[0:256, :]
    q = ic * (h_core[...] - yc)
    umat[...] = part[...] + adjoint_rows(q, wt, (e_core,), (dcore,), ua, norm)
    adjoint_finish(bands[1], umat, adj)
    for k, a in enumerate((a0, a1, a2, a3)):
        a[...] = adj[:, scal[1] ^ k].astype(BF16)

    def total(m, carry):
        gg, cg = carry
        c = cm[m].astype(F32)
        g = c + adj[m]
        adj[m] = g
        return gg + jnp.sum(g * g, axis=0), cg + jnp.sum(c * g, axis=0)

    zero = jnp.zeros((8, 256), F32)
    gg, cg = lax.fori_loop(0, share, total, (zero, zero), unroll=2)

    def rows_of(r):
        some = GRP // 32
        return adj[r // 32 : r // 32 + some].reshape(GRP, 256)

    smooth_rows(rows_of, False, bands[0], avb)
    hx_core[0:16, :] = obs_rows(avb, umat, (e_core,), (dcore,), w, dxs, norm)
    hx_core[16:24, :] = jnp.zeros((8, 256), F32)
    hx_core[16:17, :] = jnp.sum(s0[...], axis=0, keepdims=True)
    hx_core[17:18, :] = jnp.sum(gg, axis=0, keepdims=True)
    hx_core[18:19, :] = jnp.sum(cg, axis=0, keepdims=True)


def misfit_kernel(h1_oe, h1_core, obs, x_core, out):
    ic, yc = obs_of(x_core)
    own = h1_oe[0:16, :] - obs[1]
    core = h1_core[...] - yc
    qo = obs[0] * own
    qc = ic * core
    out[0:16, :] = qo
    out[16:32, :] = qc
    out[32:40, :] = jnp.zeros((8, 256), F32)
    out[32:33, :] = jnp.sum(qo * own, axis=0, keepdims=True) + jnp.sum(
        qc * core, axis=0, keepdims=True
    )


def sums_kernel(hs, h_core, misfit, obs, x_core, out):
    ic, _ = obs_of(x_core)
    do, dc = hs[0:16, :], h_core[...]

    def both(own, core):
        return jnp.sum(own, axis=0, keepdims=True) + jnp.sum(core, axis=0, keepdims=True)

    out[...] = hs[32:40, :]
    out[3:4, :] = misfit[32:33, :]
    out[4:5, :] = both(misfit[0:16, :] * do, misfit[16:32, :] * dc)
    out[5:6, :] = both(obs[0] * do * do, ic * dc * dc)


def third_kernel(
    norm, scal, part, h_core, e_core, x_core, bands, wt, a0, a1, a2, a3, adj, ua, umat
):
    ic, _ = obs_of(x_core)
    umat[...] = part[...] + adjoint_rows(
        ic * h_core[...], wt, (e_core,), (x_core[0:256, :],), ua, norm
    )
    adjoint_finish(bands[1], umat, adj)
    for k, a in enumerate((a0, a1, a2, a3)):
        a[...] = adj[:, scal[1] ^ k].astype(BF16)


def grad_first_kernel(scal, ctl, a0, a1, a2, a3, out):
    share = a0.shape[0]
    for k, a in enumerate((a0, a1, a2, a3)):
        at = pl.ds(share * (scal[2] ^ k), share)
        out[at] = ctl[at] + a[...].astype(F32)


def grad_second_kernel(
    count, scal, ctl, a0, a1, a2, a3, b0, b1, b2, b3, sums, out, costs
):
    tot = jnp.sum(sums[...], axis=1, keepdims=True)
    cc, gg, cg = tot[0:1], tot[1:2], tot[2:3]
    dd, qd, rd = tot[3:4], tot[4:5], tot[5:6]
    tau = STEP / jnp.sqrt(gg / count + 1e-06)
    first = (0.5 * cc + 0.5 * dd) / count
    second = 0.5 * (cc - 2.0 * tau * cg + tau * tau * gg) + 0.5 * (
        dd - 2.0 * tau * qd + tau * tau * rd
    )
    tb = jnp.broadcast_to(tau, (8, 256))
    share = a0.shape[0]
    for k, (a, b) in enumerate(zip((a0, a1, a2, a3), (b0, b1, b2, b3))):
        base = share * (scal[2] ^ k)

        def body(m, _, a=a, b=b, base=base):
            g = ctl[base + m] + a[m].astype(F32)
            out[base + m] = g - tb * (g + b[m].astype(F32))
            return 0

        lax.fori_loop(0, share, body, 0, unroll=10)
    costs[0] = first[0, 0]
    costs[1] = (second / count)[0, 0]


def make_pairs(tiles, levs):
    def flat(t, g):
        return t * levs + g

    def zh(t):
        return (t >> 3) & 1

    edge = []
    for t in range(tiles):
        e = (t + 1) % tiles if t & 1 else (t - 1) % tiles
        for g in range(levs):
            edge.append((flat(t, g), flat(e, g if zh(t) == zh(e) else g ^ 2)))
    far = [(flat(t, g), flat(t ^ 8, g ^ 2)) for t in range(tiles) for g in range(levs)]

    def tile_xor(k):
        return [(t, t ^ k) for t in range(tiles)]

    def lev_xor(k):
        return [(g, g ^ k) for g in range(levs)]

    return edge, far, tile_xor, lev_xor


def per_device(
    control, ensemble, loc_blocks, neighbours, vert_band, channel_weights, innovation, inv_error
):
    members, ldev, pdev = control.shape
    tiles = lax.axis_size("tile")
    levs = lax.axis_size("lev")
    lev = levs * ldev
    share = members // levs
    rows = share * lev
    norm = 1.0 / math.sqrt(members - 1)
    edge, far, tile_xor, lev_xor = make_pairs(tiles, levs)
    both = ("tile", "lev")
    tile_pos = lax.axis_index("tile").astype(jnp.int32)
    lev_pos = lax.axis_index("lev").astype(jnp.int32)
    mset = lev_pos ^ (2 * ((tile_pos >> 3) & 1))
    scal = jnp.stack([tile_pos, lev_pos, mset, mset])

    def swap_core(x):
        return lax.ppermute(x, "tile", tile_xor(1))

    def swap_edge(x):
        return lax.ppermute(x, both, edge)

    def shuffle(parts):
        return [parts[0]] + [lax.ppermute(parts[k], "lev", lev_xor(k)) for k in range(1, 4)]

    def sum4(x, axis, pairs, steps):
        one, two, three = (
            lax.ppermute(x, axis, pairs(k)) for k in steps
        )
        return (x + one) + (two + three)

    chunk = sds((share, ldev, pdev), BF16)
    hbm = pl.BlockSpec(memory_space=pltpu.HBM)

    def far_off(x):
        return pltpu.with_memory_space_constraint(x, pltpu.HBM)

    eparts = call(
        pack_ens_kernel, [chunk] * 4, (scal, far_off(ensemble)), 1,
        [pltpu.SemaphoreType.DMA((4,))],
        specs=[SM, hbm],
    )
    eparts = shuffle(eparts)
    obs_n = channel_weights.shape[0]
    d_own, x_core, x_edge, bands, obs_own = call(
        densify_kernel,
        [
            sds((256, 256), BF16), sds((352, 256), BF16), sds((352, 256), BF16),
            sds((2, GRP, 3 * GRP), BF16), sds((2, obs_n, pdev), F32),
        ],
        (
            scal, far_off(neighbours), far_off(loc_blocks), far_off(inv_error),
            far_off(innovation), far_off(vert_band.T),
        ),
        1,
        [
            pltpu.VMEM((12, 128, 128), F32), pltpu.VMEM(loc_blocks.shape, BF16),
            pltpu.VMEM((GRP, GRP), F32), pltpu.VMEM((16, 128), F32),
            pltpu.SMEM(neighbours.shape, jnp.int32), pltpu.VMEM((NS, lev), F32),
            pltpu.SemaphoreType.DMA((6,)),
        ],
        specs=[SM, hbm, hbm, hbm, hbm, hbm],
    )
    wt_own = jnp.pad(channel_weights.T, ((0, 0), (0, pdev - channel_weights.shape[0])))
    packed = call(
        pack_ctl_kernel,
        [sds((share + 3, ldev, pdev), BF16)] * 4 + [sds((ldev, pdev), F32)],
        (scal, control, wt_own),
        1,
    )
    s0 = packed[4]
    x_edge = swap_edge(x_edge)
    x_core = swap_core(x_core)
    field = sds((share, levs, ldev, pdev), BF16)
    (e_own,) = call(assemble_kernel, [field], (scal, *eparts), 1)
    e_edge = swap_edge(e_own)
    e_core = swap_core(e_own)
    cparts = shuffle(packed[:4])

    umat = pltpu.VMEM((rows, pdev), F32)
    half = pltpu.VMEM((rows, pdev), BF16)
    full = pltpu.VMEM((share, levs, ldev, pdev), F32)
    obs = channel_weights.shape[0]
    mm = 2 * rows * pdev * pdev
    row = sds((obs, pdev), F32)
    flat = sds((rows, pdev), BF16)
    wide = sds((rows, pdev), F32)

    def bind(fn, *given):
        def kernel(*refs):
            fn(*given, *refs)

        return kernel

    cm, avb, hx_core, hx_own, w, wt = call(
        bind(first_kernel, norm),
        [field, flat, row, row, sds((obs, 128), F32), sds((lev, 128), F32)],
        (scal, *cparts, e_own, e_core, d_own, x_core, bands),
        1,
        [full, pltpu.VMEM((128, 128), F32), umat, pltpu.VMEM((lev, 2 * pdev), F32)],
        3 * mm,
    )

    def reduce_obs(tag, core_msg, own, smooth):
        got = swap_core(core_msg)
        if own is None:
            own, edge_row = call(
                bind(own_edge_kernel, norm),
                [row, row],
                (smooth, e_own, e_edge, d_own, x_edge, w),
                0,
                [umat, pltpu.VMEM((lev, 2 * pdev), F32)],
                2 * mm,
            )
        else:
            (edge_row,) = call(
                bind(edge_kernel, norm),
                [row],
                (smooth, e_edge, x_edge, w),
                0,
                [umat, pltpu.VMEM((lev, pdev), F32)],
                mm,
            )
        mine = jnp.concatenate([own + got[:obs], edge_row], axis=0)
        other = swap_edge(mine)
        tot = mine + jnp.concatenate([other[obs:], other[:obs]], axis=0)
        if core_msg.shape[0] > obs:
            extra = core_msg[obs:] + got[obs:]
            tot = jnp.concatenate([tot, extra], axis=0)
        tot = sum4(tot, "lev", lev_xor, (1, 2, 3))
        core = swap_core(tot[:obs])
        (part,) = call(
            bind(partial_kernel, norm, tag == "a"),
            [wide],
            (tot, obs_own, e_own, e_edge, d_own, x_edge, wt),
            0,
            [half],
            2 * mm,
        )
        return tot, core, part

    h1_oe, h1_core, part = reduce_obs("a", hx_core, hx_own, avb)
    outs = call(
        bind(second_kernel, norm),
        [chunk] * 4 + [flat, sds((obs + 8, pdev), F32)],
        (scal, part, h1_core, cm, e_core, x_core, bands, w, wt, s0),
        1,
        [full, half, umat, pltpu.VMEM((lev, pdev), F32)],
        5 * mm,
    )
    aparts = shuffle(outs[:4])
    (misfit,) = call(misfit_kernel, [sds((40, pdev), F32)], (h1_oe, h1_core, obs_own, x_core), 0)
    hs, hd_core, part = reduce_obs("b", outs[5], None, outs[4])
    sums = call(sums_kernel, [sds((8, pdev), F32)], (hs, hd_core, misfit, obs_own, x_core), 0)[0]
    bparts = call(
        bind(third_kernel, norm),
        [chunk] * 4,
        (scal, part, hd_core, e_core, x_core, bands, wt),
        1,
        [full, half, umat],
        3 * mm,
    )
    bparts = shuffle(bparts)
    sums = sum4(sums, "tile", tile_xor, (2, 4, 6))
    sums = sums + lax.ppermute(sums, both, far)
    sums = sum4(sums, "tile", tile_xor, (16, 32, 48))
    whole = sds((members, ldev, pdev), F32)
    (grad_first,) = call(grad_first_kernel, [whole], (scal, control, *aparts), 1)
    count = float(members * lev * pdev * tiles)
    grad_second, costs = call(
        bind(grad_second_kernel, count),
        [whole, sds((2,), F32)],
        (scal, control, *aparts, *bparts, sums),
        1,
        out_specs=(VM, SM),
    )
    return grad_first, grad_second, costs


def solution(mesh):
    placed = (
        P(None, "lev", "tile"),
        P(None, "lev", "tile"),
        P("tile", None, None, None),
        P("tile", None),
        P(),
        P(None, "lev"),
        P(None, "tile"),
        P(None, "tile"),
    )
    return jax.shard_map(
        per_device,
        mesh=mesh,
        in_specs=placed,
        out_specs=(P(None, "lev", "tile"), P(None, "lev", "tile"), P()),
        check_vma=False,
    )
```

```python
import math

import jax
import jax.numpy as jnp
from jax import lax
from jax.experimental import pallas as pl
from jax.experimental.pallas import tpu as pltpu
from jax.sharding import PartitionSpec as P


HV = 4
NS = 2 * HV + 1
STEP = 0.5
GRP = 128
F32 = jnp.float32
BF16 = jnp.bfloat16
VM = pl.BlockSpec(memory_space=pltpu.VMEM)
SM = pl.BlockSpec(memory_space=pltpu.SMEM)


def call(body, outs, args, scalars, scratch=(), flops=0, specs=None, out_specs=None):
    if specs is None:
        specs = [SM] * scalars + [VM] * (len(args) - scalars)
    if out_specs is None:
        out_specs = tuple(VM for _ in outs)
    moved = sum(a.size * a.dtype.itemsize for a in args)
    moved += sum(math.prod(o.shape) * jnp.dtype(o.dtype).itemsize for o in outs)
    return pl.pallas_call(
        body,
        out_shape=tuple(outs),
        in_specs=specs,
        out_specs=out_specs,
        scratch_shapes=list(scratch),
        cost_estimate=pl.CostEstimate(flops=flops, bytes_accessed=moved, transcendentals=0),
        compiler_params=pltpu.CompilerParams(vmem_limit_bytes=48 * 1024 * 1024),
    )(*args)


def sds(shape, dtype):
    return jax.ShapeDtypeStruct(shape, dtype)


def split3(x):
    hi = x.astype(BF16)
    rest = x - hi.astype(F32)
    mid = rest.astype(BF16)
    lo = (rest - mid.astype(F32)).astype(BF16)
    return hi, mid, lo


def join3(hi, mid, lo):
    return (hi.astype(F32) + mid.astype(F32)) + lo.astype(F32)


def pack_ens_kernel(scal, ens, loc, inv, inn, vbt, nb, *refs):
    outs, (loc_out, obs_out, vbt_out, nb_out, sems) = refs[:4], refs[4:]
    share = outs[0].shape[0]
    moves = [(ens.at[pl.ds(share * (scal[2] ^ k), share)], outs[k]) for k in range(4)]
    moves += [
        (loc, loc_out), (inv, obs_out.at[0]), (inn, obs_out.at[1]), (vbt, vbt_out),
        (nb, nb_out),
    ]
    copies = [
        pltpu.make_async_copy(src, dst, sems.at[i]) for i, (src, dst) in enumerate(moves)
    ]
    for c in copies:
        c.start()
    for c in copies:
        c.wait()


def pack_ctl_kernel(scal, ctl, wt, *outs):
    share = outs[0].shape[0] - 3
    parts = split3(wt[...])
    for k in range(4):
        outs[k][pl.ds(0, share)] = ctl[pl.ds(share * (scal[2] ^ k), share)].astype(BF16)
        for i in range(3):
            outs[k][share + i] = parts[i]
    sq = jnp.zeros(outs[4].shape, F32)

    def body(m, acc):
        v = ctl[m]
        return acc + v * v

    outs[4][...] = lax.fori_loop(0, ctl.shape[0], body, sq, unroll=4)


def densify_kernel(
    scal, nb_near, loc, obs, vbt, d_own, x_core, x_edge, bands, acc, mat, narrow, nb, sem
):
    fetch = pltpu.make_async_copy(nb_near, nb, sem)
    fetch.start()
    narrow[...] = jnp.zeros(narrow.shape, F32)
    narrow[0:NS, 0:32] = vbt[...]
    band = narrow[...]
    band = band + pltpu.roll(band, 32, 1)
    band = band + pltpu.roll(band, 64, 1)
    row = lax.broadcasted_iota(jnp.int32, (GRP, GRP), 0)
    col = lax.broadcasted_iota(jnp.int32, (GRP, GRP), 1)
    shift = row - col
    same = (row >> 5) == (col >> 5)
    tot = jnp.zeros((GRP, GRP), F32)
    for s in range(NS):
        tot = jnp.where(same & (shift == s - HV), band[s : s + 1, :], tot)
    mat[...] = tot
    back = mat[...]
    fwd = mat[...].T
    for i, m in enumerate((fwd, back)):
        hi = m.astype(BF16)
        bands[i, :, 0:GRP] = hi
        bands[i, :, GRP : 2 * GRP] = hi
        bands[i, :, 2 * GRP : 3 * GRP] = (m - hi.astype(F32)).astype(BF16)
    tile = scal[0]
    core_rel = 2 - 2 * (tile & 1)
    acc[...] = jnp.zeros(acc.shape, F32)
    fetch.wait()
    for b in range(2):
        for j in range(loc.shape[1]):
            n = nb[b, j]
            rel = ((n >> 1) - tile + 65) & 63
            role = jnp.where(rel == 1, 0, jnp.where(rel == core_rel, 1, 2))
            slot = b * 6 + role * 2 + (n & 1)
            acc[slot] = acc[slot] + loc[b, j].astype(F32)
    for role, out in enumerate((d_own, x_core, x_edge)):
        for b in range(2):
            for h in range(2):
                out[128 * b : 128 * b + 128, 128 * h : 128 * h + 128] = acc[
                    b * 6 + role * 2 + h
                ].astype(BF16)
    for out in (x_core, x_edge):
        for i, v in enumerate(split3(obs[0]) + split3(obs[1])):
            out[256 + 16 * i : 272 + 16 * i, :] = v


def assemble_kernel(scal, e0, e1, e2, e3, out):
    for k, e in enumerate((e0, e1, e2, e3)):
        out[:, scal[1] ^ k] = e[...]


def band_apply(mat, x, exact):
    if exact:
        return jnp.dot(
            mat[:, GRP : 3 * GRP], jnp.concatenate([x, x], axis=0), preferred_element_type=F32
        )
    xh = x.astype(BF16)
    xl = (x - xh.astype(F32)).astype(BF16)
    return jnp.dot(mat, jnp.concatenate([xh, xl, xh], axis=0), preferred_element_type=F32)


def smooth_rows(src, exact, mat, avb):
    for r in range(0, avb.shape[0], GRP):
        avb[r : r + GRP, :] = band_apply(mat, src(r), exact).astype(BF16)


def obs_rows(avb, umat, ens3, dmats, w, dxs, norm):
    lev = 32
    ms = avb.shape[0] // lev
    for i, (ens, d) in enumerate(zip(ens3, dmats)):
        umat[...] = lax.dot_general(
            avb[...], d, (((1,), (1,)), ((), ())), preferred_element_type=F32
        )

        def member(m, acc):
            e = ens[m].astype(F32).reshape(lev, 256)
            return acc + e * umat[pl.ds(pl.multiple_of(lev * m, lev), lev), :]

        dx = lax.fori_loop(0, ms, member, jnp.zeros((lev, 256), F32), unroll=4)
        dxs[:, 256 * i : 256 * i + 256] = dx * norm
    return jnp.dot(
        w[:, 0:lev], dxs[...], precision=lax.Precision.HIGHEST, preferred_element_type=F32
    )


def adjoint_rows(q, wt, ens3, dmats, ua, norm):
    lev = 32
    ms = ua.shape[0] // lev
    dxa = (
        jnp.dot(wt[:, 0:16], q, precision=lax.Precision.HIGHEST, preferred_element_type=F32)
        * norm
    )
    total = None
    for i, (ens, d) in enumerate(zip(ens3, dmats)):
        mine = dxa[:, 256 * i : 256 * i + 256]

        def member(m, _, ens=ens, mine=mine):
            e = ens[m].astype(F32).reshape(lev, 256)
            ua[pl.ds(pl.multiple_of(lev * m, lev), lev), :] = (e * mine).astype(BF16)
            return 0

        lax.fori_loop(0, ms, member, 0, unroll=4)
        part = jnp.dot(ua[...], d, preferred_element_type=F32)
        total = part if total is None else total + part
    return total


def adjoint_finish(mat, umat, out):
    lev = 32
    some = GRP // lev
    for i in range(0, out.shape[0], some):
        got = band_apply(mat, umat[lev * i : lev * i + GRP, :], False)
        out[i : i + some] = got.reshape(some, 4, 8, 256)


def obs_of(x):
    return (
        join3(x[256:272, :], x[272:288, :], x[288:304, :]),
        join3(x[304:320, :], x[320:336, :], x[336:352, :]),
    )


def first_kernel(
    norm, scal, c0, c1, c2, c3, e_own, e_core, d_own, x_core, bands,
    cm, avb, hx_core, hx_own, w, wt, src, wsq, umat, dxs,
):
    share = src.shape[0]
    wsq[...] = jnp.zeros(wsq.shape, F32)
    for k, c in enumerate((c0, c1, c2, c3)):
        group = scal[1] ^ k
        val = c[pl.ds(0, share)]
        cm[:, group] = val
        src[:, group] = val.astype(F32)
        wsq[pl.ds(pl.multiple_of(8 * group, 8), 8), :] = join3(
            c[share], c[share + 1], c[share + 2]
        )[:, 0:128]
    w[...] = wsq[...].T[0:16, :]
    wt[...] = wsq[0:32, :]

    def rows_of(r):
        some = GRP // 32
        return src[r // 32 : r // 32 + some].reshape(GRP, 256).astype(BF16)

    smooth_rows(rows_of, True, bands[0], avb)
    hx = obs_rows(avb, umat, (e_own, e_core), (d_own[...], x_core[0:256, :]), w, dxs, norm)
    hx_own[...] = hx[:, 0:256]
    hx_core[...] = hx[:, 256:512]


def edge_kernel(norm, avb, e_edge, x_edge, w, hx_edge, umat, dxs):
    hx_edge[...] = obs_rows(avb, umat, (e_edge,), (x_edge[0:256, :],), w, dxs, norm)


def own_edge_kernel(norm, avb, e_own, e_edge, d_own, x_edge, w, hx_own, hx_edge, umat, dxs):
    hx = obs_rows(
        avb, umat, (e_own, e_edge), (d_own[...], x_edge[0:256, :]), w, dxs, norm
    )
    hx_own[...] = hx[:, 0:256]
    hx_edge[...] = hx[:, 256:512]


def partial_kernel(norm, affine, h_oe, obs, e_own, e_edge, d_own, x_edge, wt, out, ua):
    ie, ye = obs_of(x_edge)
    own, edge = h_oe[0:16, :], h_oe[16:32, :]
    if affine:
        own, edge = own - obs[1], edge - ye
    q = jnp.concatenate([obs[0] * own, ie * edge], axis=1)
    out[...] = adjoint_rows(
        q, wt, (e_own, e_edge), (d_own[...], x_edge[0:256, :]), ua, norm
    )


def second_kernel(
    norm, scal, part, h_core, cm, e_core, x_core, bands, w, wt, s0,
    a0, a1, a2, a3, avb, hx_core, adj, ua, umat, dxs,
):
    share = adj.shape[0]
    ic, yc = obs_of(x_core)
    dcore = x_core[0:256, :]
    q = ic * (h_core[...] - yc)
    umat[...] = part[...] + adjoint_rows(q, wt, (e_core,), (dcore,), ua, norm)
    adjoint_finish(bands[1], umat, adj)
    for k, a in enumerate((a0, a1, a2, a3)):
        a[...] = adj[:, scal[1] ^ k].astype(BF16)

    def total(m, carry):
        gg, cg = carry
        c = cm[m].astype(F32)
        g = c + adj[m]
        adj[m] = g
        return gg + jnp.sum(g * g, axis=0), cg + jnp.sum(c * g, axis=0)

    zero = jnp.zeros((8, 256), F32)
    gg, cg = lax.fori_loop(0, share, total, (zero, zero), unroll=2)

    def rows_of(r):
        some = GRP // 32
        return adj[r // 32 : r // 32 + some].reshape(GRP, 256)

    smooth_rows(rows_of, False, bands[0], avb)
    hx_core[0:16, :] = obs_rows(avb, umat, (e_core,), (dcore,), w, dxs, norm)
    hx_core[16:24, :] = jnp.zeros((8, 256), F32)
    hx_core[16:17, :] = jnp.sum(s0[...], axis=0, keepdims=True)
    hx_core[17:18, :] = jnp.sum(gg, axis=0, keepdims=True)
    hx_core[18:19, :] = jnp.sum(cg, axis=0, keepdims=True)


def misfit_kernel(h1_oe, h1_core, obs, x_core, out):
    ic, yc = obs_of(x_core)
    own = h1_oe[0:16, :] - obs[1]
    core = h1_core[...] - yc
    qo = obs[0] * own
    qc = ic * core
    out[0:16, :] = qo
    out[16:32, :] = qc
    out[32:40, :] = jnp.zeros((8, 256), F32)
    out[32:33, :] = jnp.sum(qo * own, axis=0, keepdims=True) + jnp.sum(
        qc * core, axis=0, keepdims=True
    )


def sums_kernel(hs, h_core, misfit, obs, x_core, out):
    ic, _ = obs_of(x_core)
    do, dc = hs[0:16, :], h_core[...]

    def both(own, core):
        return jnp.sum(own, axis=0, keepdims=True) + jnp.sum(core, axis=0, keepdims=True)

    out[...] = hs[32:40, :]
    out[3:4, :] = misfit[32:33, :]
    out[4:5, :] = both(misfit[0:16, :] * do, misfit[16:32, :] * dc)
    out[5:6, :] = both(obs[0] * do * do, ic * dc * dc)


def third_kernel(
    norm, scal, part, h_core, e_core, x_core, bands, wt, a0, a1, a2, a3, adj, ua, umat
):
    ic, _ = obs_of(x_core)
    umat[...] = part[...] + adjoint_rows(
        ic * h_core[...], wt, (e_core,), (x_core[0:256, :],), ua, norm
    )
    adjoint_finish(bands[1], umat, adj)
    for k, a in enumerate((a0, a1, a2, a3)):
        a[...] = adj[:, scal[1] ^ k].astype(BF16)


def grad_first_kernel(scal, ctl, a0, a1, a2, a3, out):
    share = a0.shape[0]
    for k, a in enumerate((a0, a1, a2, a3)):
        at = pl.ds(share * (scal[2] ^ k), share)
        out[at] = ctl[at] + a[...].astype(F32)


def grad_second_kernel(
    count, scal, ctl, a0, a1, a2, a3, b0, b1, b2, b3, sums, out, costs
):
    tot = jnp.sum(sums[...], axis=1, keepdims=True)
    cc, gg, cg = tot[0:1], tot[1:2], tot[2:3]
    dd, qd, rd = tot[3:4], tot[4:5], tot[5:6]
    tau = STEP / jnp.sqrt(gg / count + 1e-06)
    first = (0.5 * cc + 0.5 * dd) / count
    second = 0.5 * (cc - 2.0 * tau * cg + tau * tau * gg) + 0.5 * (
        dd - 2.0 * tau * qd + tau * tau * rd
    )
    tb = jnp.broadcast_to(tau, (8, 256))
    share = a0.shape[0]
    for k, (a, b) in enumerate(zip((a0, a1, a2, a3), (b0, b1, b2, b3))):
        base = share * (scal[2] ^ k)

        def body(m, _, a=a, b=b, base=base):
            g = ctl[base + m] + a[m].astype(F32)
            out[base + m] = g - tb * (g + b[m].astype(F32))
            return 0

        lax.fori_loop(0, share, body, 0, unroll=10)
    costs[0] = first[0, 0]
    costs[1] = (second / count)[0, 0]


def make_pairs(tiles, levs):
    def flat(t, g):
        return t * levs + g

    def zh(t):
        return (t >> 3) & 1

    edge = []
    for t in range(tiles):
        e = (t + 1) % tiles if t & 1 else (t - 1) % tiles
        for g in range(levs):
            edge.append((flat(t, g), flat(e, g if zh(t) == zh(e) else g ^ 2)))
    far = [(flat(t, g), flat(t ^ 8, g ^ 2)) for t in range(tiles) for g in range(levs)]

    def tile_xor(k):
        return [(t, t ^ k) for t in range(tiles)]

    def lev_xor(k):
        return [(g, g ^ k) for g in range(levs)]

    return edge, far, tile_xor, lev_xor


def per_device(
    control, ensemble, loc_blocks, neighbours, vert_band, channel_weights, innovation, inv_error
):
    members, ldev, pdev = control.shape
    tiles = lax.axis_size("tile")
    levs = lax.axis_size("lev")
    lev = levs * ldev
    share = members // levs
    rows = share * lev
    norm = 1.0 / math.sqrt(members - 1)
    edge, far, tile_xor, lev_xor = make_pairs(tiles, levs)
    both = ("tile", "lev")
    tile_pos = lax.axis_index("tile").astype(jnp.int32)
    lev_pos = lax.axis_index("lev").astype(jnp.int32)
    mset = lev_pos ^ (2 * ((tile_pos >> 3) & 1))
    scal = jnp.stack([tile_pos, lev_pos, mset, mset])

    def swap_core(x):
        return lax.ppermute(x, "tile", tile_xor(1))

    def swap_edge(x):
        return lax.ppermute(x, both, edge)

    def shuffle(parts):
        return [parts[0]] + [lax.ppermute(parts[k], "lev", lev_xor(k)) for k in range(1, 4)]

    def sum4(x, axis, pairs, steps):
        one, two, three = (
            lax.ppermute(x, axis, pairs(k)) for k in steps
        )
        return (x + one) + (two + three)

    chunk = sds((share, ldev, pdev), BF16)
    hbm = pl.BlockSpec(memory_space=pltpu.HBM)

    def far_off(x):
        return pltpu.with_memory_space_constraint(x, pltpu.HBM)

    obs_n = channel_weights.shape[0]
    *eparts, loc_near, obs_own, vbt, nb_near = call(
        pack_ens_kernel,
        [chunk] * 4
        + [
            sds(loc_blocks.shape, BF16), sds((2, obs_n, pdev), F32),
            sds(vert_band.shape[::-1], F32), sds(neighbours.shape, jnp.int32),
        ],
        (
            scal, far_off(ensemble), far_off(loc_blocks), far_off(inv_error),
            far_off(innovation), far_off(vert_band.T), far_off(neighbours),
        ),
        1,
        [pltpu.SemaphoreType.DMA((9,))],
        specs=[SM, hbm, hbm, hbm, hbm, hbm, hbm],
    )
    eparts = shuffle(eparts)
    d_own, x_core, x_edge, bands = call(
        densify_kernel,
        [
            sds((256, 256), BF16), sds((352, 256), BF16), sds((352, 256), BF16),
            sds((2, GRP, 3 * GRP), BF16),
        ],
        (scal, nb_near, loc_near, obs_own, vbt),
        1,
        [
            pltpu.VMEM((12, 128, 128), F32), pltpu.VMEM((GRP, GRP), F32),
            pltpu.VMEM((16, 128), F32), pltpu.SMEM(neighbours.shape, jnp.int32),
            pltpu.SemaphoreType.DMA,
        ],
    )
    wt_own = jnp.pad(channel_weights.T, ((0, 0), (0, pdev - channel_weights.shape[0])))
    packed = call(
        pack_ctl_kernel,
        [sds((share + 3, ldev, pdev), BF16)] * 4 + [sds((ldev, pdev), F32)],
        (scal, control, wt_own),
        1,
    )
    s0 = packed[4]
    x_edge = swap_edge(x_edge)
    x_core = swap_core(x_core)
    field = sds((share, levs, ldev, pdev), BF16)
    (e_own,) = call(assemble_kernel, [field], (scal, *eparts), 1)
    e_edge = swap_edge(e_own)
    e_core = swap_core(e_own)
    cparts = shuffle(packed[:4])

    umat = pltpu.VMEM((rows, pdev), F32)
    half = pltpu.VMEM((rows, pdev), BF16)
    full = pltpu.VMEM((share, levs, ldev, pdev), F32)
    obs = channel_weights.shape[0]
    mm = 2 * rows * pdev * pdev
    row = sds((obs, pdev), F32)
    flat = sds((rows, pdev), BF16)
    wide = sds((rows, pdev), F32)

    def bind(fn, *given):
        def kernel(*refs):
            fn(*given, *refs)

        return kernel

    cm, avb, hx_core, hx_own, w, wt = call(
        bind(first_kernel, norm),
        [field, flat, row, row, sds((obs, 128), F32), sds((lev, 128), F32)],
        (scal, *cparts, e_own, e_core, d_own, x_core, bands),
        1,
        [full, pltpu.VMEM((128, 128), F32), umat, pltpu.VMEM((lev, 2 * pdev), F32)],
        3 * mm,
    )

    def reduce_obs(tag, core_msg, own, smooth):
        got = swap_core(core_msg)
        if own is None:
            own, edge_row = call(
                bind(own_edge_kernel, norm),
                [row, row],
                (smooth, e_own, e_edge, d_own, x_edge, w),
                0,
                [umat, pltpu.VMEM((lev, 2 * pdev), F32)],
                2 * mm,
            )
        else:
            (edge_row,) = call(
                bind(edge_kernel, norm),
                [row],
                (smooth, e_edge, x_edge, w),
                0,
                [umat, pltpu.VMEM((lev, pdev), F32)],
                mm,
            )
        mine = jnp.concatenate([own + got[:obs], edge_row], axis=0)
        other = swap_edge(mine)
        tot = mine + jnp.concatenate([other[obs:], other[:obs]], axis=0)
        if core_msg.shape[0] > obs:
            extra = core_msg[obs:] + got[obs:]
            tot = jnp.concatenate([tot, extra], axis=0)
        tot = sum4(tot, "lev", lev_xor, (1, 2, 3))
        core = swap_core(tot[:obs])
        (part,) = call(
            bind(partial_kernel, norm, tag == "a"),
            [wide],
            (tot, obs_own, e_own, e_edge, d_own, x_edge, wt),
            0,
            [half],
            2 * mm,
        )
        return tot, core, part

    h1_oe, h1_core, part = reduce_obs("a", hx_core, hx_own, avb)
    outs = call(
        bind(second_kernel, norm),
        [chunk] * 4 + [flat, sds((obs + 8, pdev), F32)],
        (scal, part, h1_core, cm, e_core, x_core, bands, w, wt, s0),
        1,
        [full, half, umat, pltpu.VMEM((lev, pdev), F32)],
        5 * mm,
    )
    aparts = shuffle(outs[:4])
    (misfit,) = call(misfit_kernel, [sds((40, pdev), F32)], (h1_oe, h1_core, obs_own, x_core), 0)
    hs, hd_core, part = reduce_obs("b", outs[5], None, outs[4])
    sums = call(sums_kernel, [sds((8, pdev), F32)], (hs, hd_core, misfit, obs_own, x_core), 0)[0]
    bparts = call(
        bind(third_kernel, norm),
        [chunk] * 4,
        (scal, part, hd_core, e_core, x_core, bands, wt),
        1,
        [full, half, umat],
        3 * mm,
    )
    bparts = shuffle(bparts)
    sums = sums + lax.ppermute(sums, both, far)
    sums = sum4(sums, "tile", tile_xor, (2, 4, 6))
    sums = sum4(sums, "tile", tile_xor, (16, 32, 48))
    whole = sds((members, ldev, pdev), F32)
    (grad_first,) = call(grad_first_kernel, [whole], (scal, control, *aparts), 1)
    count = float(members * lev * pdev * tiles)
    grad_second, costs = call(
        bind(grad_second_kernel, count),
        [whole, sds((2,), F32)],
        (scal, control, *aparts, *bparts, sums),
        1,
        out_specs=(VM, SM),
    )
    return grad_first, grad_second, costs


def solution(mesh):
    placed = (
        P(None, "lev", "tile"),
        P(None, "lev", "tile"),
        P("tile", None, None, None),
        P("tile", None),
        P(),
        P(None, "lev"),
        P(None, "tile"),
        P(None, "tile"),
    )
    return jax.shard_map(
        per_device,
        mesh=mesh,
        in_specs=placed,
        out_specs=(P(None, "lev", "tile"), P(None, "lev", "tile"), P()),
        check_vma=False,
    )
```

```python
import math

import jax
import jax.numpy as jnp
from jax import lax
from jax.experimental import pallas as pl
from jax.experimental.pallas import tpu as pltpu
from jax.sharding import PartitionSpec as P


HV = 4
NS = 2 * HV + 1
STEP = 0.5
GRP = 128
F32 = jnp.float32
BF16 = jnp.bfloat16
VM = pl.BlockSpec(memory_space=pltpu.VMEM)
SM = pl.BlockSpec(memory_space=pltpu.SMEM)


def call(body, outs, args, scalars, scratch=(), flops=0, specs=None, out_specs=None):
    if specs is None:
        specs = [SM] * scalars + [VM] * (len(args) - scalars)
    if out_specs is None:
        out_specs = tuple(VM for _ in outs)
    moved = sum(a.size * a.dtype.itemsize for a in args)
    moved += sum(math.prod(o.shape) * jnp.dtype(o.dtype).itemsize for o in outs)
    return pl.pallas_call(
        body,
        out_shape=tuple(outs),
        in_specs=specs,
        out_specs=out_specs,
        scratch_shapes=list(scratch),
        cost_estimate=pl.CostEstimate(flops=flops, bytes_accessed=moved, transcendentals=0),
        compiler_params=pltpu.CompilerParams(vmem_limit_bytes=48 * 1024 * 1024),
    )(*args)


def sds(shape, dtype):
    return jax.ShapeDtypeStruct(shape, dtype)


def split3(x):
    hi = x.astype(BF16)
    rest = x - hi.astype(F32)
    mid = rest.astype(BF16)
    lo = (rest - mid.astype(F32)).astype(BF16)
    return hi, mid, lo


def join3(hi, mid, lo):
    return (hi.astype(F32) + mid.astype(F32)) + lo.astype(F32)


def pack_ens_kernel(scal, ens, loc, inv, inn, vbt, nb, *refs):
    outs, (loc_out, obs_out, vbt_out, nb_out, sems) = refs[:4], refs[4:]
    share = outs[0].shape[0]
    moves = [(ens.at[pl.ds(share * (scal[2] ^ k), share)], outs[k]) for k in range(4)]
    moves += [
        (loc, loc_out), (inv, obs_out.at[0]), (inn, obs_out.at[1]), (vbt, vbt_out),
        (nb, nb_out),
    ]
    copies = [
        pltpu.make_async_copy(src, dst, sems.at[i]) for i, (src, dst) in enumerate(moves)
    ]
    for c in copies:
        c.start()
    for c in copies:
        c.wait()


def pack_ctl_kernel(scal, ctl, wt, *outs):
    share = outs[0].shape[0] - 3
    parts = split3(wt[...])
    for k in range(4):
        outs[k][pl.ds(0, share)] = ctl[pl.ds(share * (scal[2] ^ k), share)].astype(BF16)
        for i in range(3):
            outs[k][share + i] = parts[i]
    sq = jnp.zeros(outs[4].shape, F32)

    def body(m, acc):
        v = ctl[m]
        return acc + v * v

    outs[4][...] = lax.fori_loop(0, ctl.shape[0], body, sq, unroll=4)


def densify_kernel(
    scal, nb_near, loc, obs, vbt, d_own, x_core, x_edge, bands, acc, mat, narrow, nb, sem
):
    fetch = pltpu.make_async_copy(nb_near, nb, sem)
    fetch.start()
    narrow[...] = jnp.zeros(narrow.shape, F32)
    narrow[0:NS, 0:32] = vbt[...]
    band = narrow[...]
    band = band + pltpu.roll(band, 32, 1)
    band = band + pltpu.roll(band, 64, 1)
    row = lax.broadcasted_iota(jnp.int32, (GRP, GRP), 0)
    col = lax.broadcasted_iota(jnp.int32, (GRP, GRP), 1)
    shift = row - col
    same = (row >> 5) == (col >> 5)
    tot = jnp.zeros((GRP, GRP), F32)
    for s in range(NS):
        tot = jnp.where(same & (shift == s - HV), band[s : s + 1, :], tot)
    mat[...] = tot
    back = mat[...]
    fwd = mat[...].T
    for i, m in enumerate((fwd, back)):
        hi = m.astype(BF16)
        bands[i, :, 0:GRP] = hi
        bands[i, :, GRP : 2 * GRP] = hi
        bands[i, :, 2 * GRP : 3 * GRP] = (m - hi.astype(F32)).astype(BF16)
    tile = scal[0]
    core_rel = 2 - 2 * (tile & 1)
    acc[...] = jnp.zeros(acc.shape, F32)
    fetch.wait()
    for b in range(2):
        for j in range(loc.shape[1]):
            n = nb[b, j]
            rel = ((n >> 1) - tile + 65) & 63
            role = jnp.where(rel == 1, 0, jnp.where(rel == core_rel, 1, 2))
            slot = b * 6 + role * 2 + (n & 1)
            acc[slot] = acc[slot] + loc[b, j].astype(F32)
    for role, out in enumerate((d_own, x_core, x_edge)):
        for b in range(2):
            for h in range(2):
                out[128 * b : 128 * b + 128, 128 * h : 128 * h + 128] = acc[
                    b * 6 + role * 2 + h
                ].astype(BF16)
    for out in (x_core, x_edge):
        for i, v in enumerate(split3(obs[0]) + split3(obs[1])):
            out[256 + 16 * i : 272 + 16 * i, :] = v


def assemble_kernel(scal, e0, e1, e2, e3, out):
    for k, e in enumerate((e0, e1, e2, e3)):
        out[:, scal[1] ^ k] = e[...]


def band_apply(mat, x, exact):
    if exact:
        return jnp.dot(
            mat[:, GRP : 3 * GRP], jnp.concatenate([x, x], axis=0), preferred_element_type=F32
        )
    xh = x.astype(BF16)
    xl = (x - xh.astype(F32)).astype(BF16)
    return jnp.dot(mat, jnp.concatenate([xh, xl, xh], axis=0), preferred_element_type=F32)


def channel_dot(w, x):
    hi = x.astype(BF16)
    lo = (x - hi.astype(F32)).astype(BF16)
    return jnp.dot(w, jnp.concatenate([hi, lo, hi], axis=0), preferred_element_type=F32)


def side_by_side(w, width):
    hi = w.astype(BF16).astype(F32)
    lo = w - hi
    return (hi + pltpu.roll(hi, width, 1) + pltpu.roll(lo, 2 * width, 1)).astype(BF16)


def smooth_rows(src, exact, mat, avb):
    for r in range(0, avb.shape[0], GRP):
        avb[r : r + GRP, :] = band_apply(mat, src(r), exact).astype(BF16)


def obs_rows(avb, umat, ens3, dmats, w, dxs, norm):
    lev = 32
    ms = avb.shape[0] // lev
    for i, (ens, d) in enumerate(zip(ens3, dmats)):
        umat[...] = lax.dot_general(
            avb[...], d, (((1,), (1,)), ((), ())), preferred_element_type=F32
        )

        def member(m, acc):
            e = ens[m].astype(F32).reshape(lev, 256)
            return acc + e * umat[pl.ds(pl.multiple_of(lev * m, lev), lev), :]

        dx = lax.fori_loop(0, ms, member, jnp.zeros((lev, 256), F32), unroll=4)
        dxs[:, 256 * i : 256 * i + 256] = dx * norm
    return channel_dot(w[:, 0 : 3 * lev], dxs[...])


def adjoint_rows(q, wt, ens3, dmats, ua, norm):
    lev = 32
    ms = ua.shape[0] // lev
    dxa = channel_dot(wt[:, 0:48], q) * norm
    total = None
    for i, (ens, d) in enumerate(zip(ens3, dmats)):
        mine = dxa[:, 256 * i : 256 * i + 256]

        def member(m, _, ens=ens, mine=mine):
            e = ens[m].astype(F32).reshape(lev, 256)
            ua[pl.ds(pl.multiple_of(lev * m, lev), lev), :] = (e * mine).astype(BF16)
            return 0

        lax.fori_loop(0, ms, member, 0, unroll=4)
        part = jnp.dot(ua[...], d, preferred_element_type=F32)
        total = part if total is None else total + part
    return total


def adjoint_finish(mat, umat, out):
    lev = 32
    some = GRP // lev
    for i in range(0, out.shape[0], some):
        got = band_apply(mat, umat[lev * i : lev * i + GRP, :], False)
        out[i : i + some] = got.reshape(some, 4, 8, 256)


def obs_of(x):
    return (
        join3(x[256:272, :], x[272:288, :], x[288:304, :]),
        join3(x[304:320, :], x[320:336, :], x[336:352, :]),
    )


def first_kernel(
    norm, scal, c0, c1, c2, c3, e_own, e_core, d_own, x_core, bands,
    cm, avb, hx_core, hx_own, w, wt, src, wsq, umat, dxs,
):
    share = src.shape[0]
    wsq[...] = jnp.zeros(wsq.shape, F32)
    for k, c in enumerate((c0, c1, c2, c3)):
        group = scal[1] ^ k
        val = c[pl.ds(0, share)]
        cm[:, group] = val
        src[:, group] = val.astype(F32)
        wsq[pl.ds(pl.multiple_of(8 * group, 8), 8), :] = join3(
            c[share], c[share + 1], c[share + 2]
        )[:, 0:128]
    w[...] = side_by_side(wsq[...].T[0:16, :], 32)
    wt[...] = side_by_side(wsq[0:32, :], 16)

    def rows_of(r):
        some = GRP // 32
        return src[r // 32 : r // 32 + some].reshape(GRP, 256).astype(BF16)

    smooth_rows(rows_of, True, bands[0], avb)
    hx = obs_rows(avb, umat, (e_own, e_core), (d_own[...], x_core[0:256, :]), w, dxs, norm)
    hx_own[...] = hx[:, 0:256]
    hx_core[...] = hx[:, 256:512]


def edge_kernel(norm, avb, e_edge, x_edge, w, hx_edge, umat, dxs):
    hx_edge[...] = obs_rows(avb, umat, (e_edge,), (x_edge[0:256, :],), w, dxs, norm)


def own_edge_kernel(norm, avb, e_own, e_edge, d_own, x_edge, w, hx_own, hx_edge, umat, dxs):
    hx = obs_rows(
        avb, umat, (e_own, e_edge), (d_own[...], x_edge[0:256, :]), w, dxs, norm
    )
    hx_own[...] = hx[:, 0:256]
    hx_edge[...] = hx[:, 256:512]


def partial_kernel(norm, affine, h_oe, obs, e_own, e_edge, d_own, x_edge, wt, out, ua):
    ie, ye = obs_of(x_edge)
    own, edge = h_oe[0:16, :], h_oe[16:32, :]
    if affine:
        own, edge = own - obs[1], edge - ye
    q = jnp.concatenate([obs[0] * own, ie * edge], axis=1)
    out[...] = adjoint_rows(
        q, wt, (e_own, e_edge), (d_own[...], x_edge[0:256, :]), ua, norm
    )


def second_kernel(
    norm, scal, part, h_core, cm, e_core, x_core, bands, w, wt, s0,
    a0, a1, a2, a3, avb, hx_core, adj, ua, umat, dxs,
):
    share = adj.shape[0]
    ic, yc = obs_of(x_core)
    dcore = x_core[0:256, :]
    q = ic * (h_core[...] - yc)
    umat[...] = part[...] + adjoint_rows(q, wt, (e_core,), (dcore,), ua, norm)
    adjoint_finish(bands[1], umat, adj)
    for k, a in enumerate((a0, a1, a2, a3)):
        a[...] = adj[:, scal[1] ^ k].astype(BF16)

    def total(m, carry):
        gg, cg = carry
        c = cm[m].astype(F32)
        g = c + adj[m]
        adj[m] = g
        return gg + jnp.sum(g * g, axis=0), cg + jnp.sum(c * g, axis=0)

    zero = jnp.zeros((8, 256), F32)
    gg, cg = lax.fori_loop(0, share, total, (zero, zero), unroll=2)

    def rows_of(r):
        some = GRP // 32
        return adj[r // 32 : r // 32 + some].reshape(GRP, 256)

    smooth_rows(rows_of, False, bands[0], avb)
    hx_core[0:16, :] = obs_rows(avb, umat, (e_core,), (dcore,), w, dxs, norm)
    hx_core[16:24, :] = jnp.zeros((8, 256), F32)
    hx_core[16:17, :] = jnp.sum(s0[...], axis=0, keepdims=True)
    hx_core[17:18, :] = jnp.sum(gg, axis=0, keepdims=True)
    hx_core[18:19, :] = jnp.sum(cg, axis=0, keepdims=True)


def misfit_kernel(h1_oe, h1_core, obs, x_core, out):
    ic, yc = obs_of(x_core)
    own = h1_oe[0:16, :] - obs[1]
    core = h1_core[...] - yc
    qo = obs[0] * own
    qc = ic * core
    out[0:16, :] = qo
    out[16:32, :] = qc
    out[32:40, :] = jnp.zeros((8, 256), F32)
    out[32:33, :] = jnp.sum(qo * own, axis=0, keepdims=True) + jnp.sum(
        qc * core, axis=0, keepdims=True
    )


def sums_kernel(hs, h_core, misfit, obs, x_core, out):
    ic, _ = obs_of(x_core)
    do, dc = hs[0:16, :], h_core[...]

    def both(own, core):
        return jnp.sum(own, axis=0, keepdims=True) + jnp.sum(core, axis=0, keepdims=True)

    out[...] = hs[32:40, :]
    out[3:4, :] = misfit[32:33, :]
    out[4:5, :] = both(misfit[0:16, :] * do, misfit[16:32, :] * dc)
    out[5:6, :] = both(obs[0] * do * do, ic * dc * dc)


def third_kernel(
    norm, scal, part, h_core, e_core, x_core, bands, wt, a0, a1, a2, a3, adj, ua, umat
):
    ic, _ = obs_of(x_core)
    umat[...] = part[...] + adjoint_rows(
        ic * h_core[...], wt, (e_core,), (x_core[0:256, :],), ua, norm
    )
    adjoint_finish(bands[1], umat, adj)
    for k, a in enumerate((a0, a1, a2, a3)):
        a[...] = adj[:, scal[1] ^ k].astype(BF16)


def grad_first_kernel(scal, ctl, a0, a1, a2, a3, out):
    share = a0.shape[0]
    for k, a in enumerate((a0, a1, a2, a3)):
        at = pl.ds(share * (scal[2] ^ k), share)
        out[at] = ctl[at] + a[...].astype(F32)


def grad_second_kernel(
    count, scal, ctl, a0, a1, a2, a3, b0, b1, b2, b3, sums, out, costs
):
    tot = jnp.sum(sums[...], axis=1, keepdims=True)
    cc, gg, cg = tot[0:1], tot[1:2], tot[2:3]
    dd, qd, rd = tot[3:4], tot[4:5], tot[5:6]
    tau = STEP / jnp.sqrt(gg / count + 1e-06)
    first = (0.5 * cc + 0.5 * dd) / count
    second = 0.5 * (cc - 2.0 * tau * cg + tau * tau * gg) + 0.5 * (
        dd - 2.0 * tau * qd + tau * tau * rd
    )
    tb = jnp.broadcast_to(tau, (8, 256))
    share = a0.shape[0]
    for k, (a, b) in enumerate(zip((a0, a1, a2, a3), (b0, b1, b2, b3))):
        base = share * (scal[2] ^ k)

        def body(m, _, a=a, b=b, base=base):
            g = ctl[base + m] + a[m].astype(F32)
            out[base + m] = g - tb * (g + b[m].astype(F32))
            return 0

        lax.fori_loop(0, share, body, 0, unroll=10)
    costs[0] = first[0, 0]
    costs[1] = (second / count)[0, 0]


def make_pairs(tiles, levs):
    def flat(t, g):
        return t * levs + g

    def zh(t):
        return (t >> 3) & 1

    edge = []
    for t in range(tiles):
        e = (t + 1) % tiles if t & 1 else (t - 1) % tiles
        for g in range(levs):
            edge.append((flat(t, g), flat(e, g if zh(t) == zh(e) else g ^ 2)))
    far = [(flat(t, g), flat(t ^ 8, g ^ 2)) for t in range(tiles) for g in range(levs)]

    def tile_xor(k):
        return [(t, t ^ k) for t in range(tiles)]

    def lev_xor(k):
        return [(g, g ^ k) for g in range(levs)]

    return edge, far, tile_xor, lev_xor


def per_device(
    control, ensemble, loc_blocks, neighbours, vert_band, channel_weights, innovation, inv_error
):
    members, ldev, pdev = control.shape
    tiles = lax.axis_size("tile")
    levs = lax.axis_size("lev")
    lev = levs * ldev
    share = members // levs
    rows = share * lev
    norm = 1.0 / math.sqrt(members - 1)
    edge, far, tile_xor, lev_xor = make_pairs(tiles, levs)
    both = ("tile", "lev")
    tile_pos = lax.axis_index("tile").astype(jnp.int32)
    lev_pos = lax.axis_index("lev").astype(jnp.int32)
    mset = lev_pos ^ (2 * ((tile_pos >> 3) & 1))
    scal = jnp.stack([tile_pos, lev_pos, mset, mset])

    def swap_core(x):
        return lax.ppermute(x, "tile", tile_xor(1))

    def swap_edge(x):
        return lax.ppermute(x, both, edge)

    def shuffle(parts):
        return [parts[0]] + [lax.ppermute(parts[k], "lev", lev_xor(k)) for k in range(1, 4)]

    def sum4(x, axis, pairs, steps):
        one, two, three = (
            lax.ppermute(x, axis, pairs(k)) for k in steps
        )
        return (x + one) + (two + three)

    chunk = sds((share, ldev, pdev), BF16)
    hbm = pl.BlockSpec(memory_space=pltpu.HBM)

    def far_off(x):
        return pltpu.with_memory_space_constraint(x, pltpu.HBM)

    obs_n = channel_weights.shape[0]
    *eparts, loc_near, obs_own, vbt, nb_near = call(
        pack_ens_kernel,
        [chunk] * 4
        + [
            sds(loc_blocks.shape, BF16), sds((2, obs_n, pdev), F32),
            sds(vert_band.shape[::-1], F32), sds(neighbours.shape, jnp.int32),
        ],
        (
            scal, far_off(ensemble), far_off(loc_blocks), far_off(inv_error),
            far_off(innovation), far_off(vert_band.T), far_off(neighbours),
        ),
        1,
        [pltpu.SemaphoreType.DMA((9,))],
        specs=[SM, hbm, hbm, hbm, hbm, hbm, hbm],
    )
    eparts = shuffle(eparts)
    d_own, x_core, x_edge, bands = call(
        densify_kernel,
        [
            sds((256, 256), BF16), sds((352, 256), BF16), sds((352, 256), BF16),
            sds((2, GRP, 3 * GRP), BF16),
        ],
        (scal, nb_near, loc_near, obs_own, vbt),
        1,
        [
            pltpu.VMEM((12, 128, 128), F32), pltpu.VMEM((GRP, GRP), F32),
            pltpu.VMEM((16, 128), F32), pltpu.SMEM(neighbours.shape, jnp.int32),
            pltpu.SemaphoreType.DMA,
        ],
    )
    wt_own = jnp.pad(channel_weights.T, ((0, 0), (0, pdev - channel_weights.shape[0])))
    packed = call(
        pack_ctl_kernel,
        [sds((share + 3, ldev, pdev), BF16)] * 4 + [sds((ldev, pdev), F32)],
        (scal, control, wt_own),
        1,
    )
    s0 = packed[4]
    x_edge = swap_edge(x_edge)
    x_core = swap_core(x_core)
    field = sds((share, levs, ldev, pdev), BF16)
    (e_own,) = call(assemble_kernel, [field], (scal, *eparts), 1)
    e_edge = swap_edge(e_own)
    e_core = swap_core(e_own)
    cparts = shuffle(packed[:4])

    umat = pltpu.VMEM((rows, pdev), F32)
    half = pltpu.VMEM((rows, pdev), BF16)
    full = pltpu.VMEM((share, levs, ldev, pdev), F32)
    obs = channel_weights.shape[0]
    mm = 2 * rows * pdev * pdev
    row = sds((obs, pdev), F32)
    flat = sds((rows, pdev), BF16)
    wide = sds((rows, pdev), F32)

    def bind(fn, *given):
        def kernel(*refs):
            fn(*given, *refs)

        return kernel

    cm, avb, hx_core, hx_own, w, wt = call(
        bind(first_kernel, norm),
        [field, flat, row, row, sds((obs, 128), BF16), sds((lev, 128), BF16)],
        (scal, *cparts, e_own, e_core, d_own, x_core, bands),
        1,
        [full, pltpu.VMEM((128, 128), F32), umat, pltpu.VMEM((lev, 2 * pdev), F32)],
        3 * mm,
    )

    def reduce_obs(tag, core_msg, own, smooth):
        got = swap_core(core_msg)
        if own is None:
            own, edge_row = call(
                bind(own_edge_kernel, norm),
                [row, row],
                (smooth, e_own, e_edge, d_own, x_edge, w),
                0,
                [umat, pltpu.VMEM((lev, 2 * pdev), F32)],
                2 * mm,
            )
        else:
            (edge_row,) = call(
                bind(edge_kernel, norm),
                [row],
                (smooth, e_edge, x_edge, w),
                0,
                [umat, pltpu.VMEM((lev, pdev), F32)],
                mm,
            )
        mine = jnp.concatenate([own + got[:obs], edge_row], axis=0)
        other = swap_edge(mine)
        tot = mine + jnp.concatenate([other[obs:], other[:obs]], axis=0)
        if core_msg.shape[0] > obs:
            extra = core_msg[obs:] + got[obs:]
            tot = jnp.concatenate([tot, extra], axis=0)
        tot = sum4(tot, "lev", lev_xor, (1, 2, 3))
        core = swap_core(tot[:obs])
        (part,) = call(
            bind(partial_kernel, norm, tag == "a"),
            [wide],
            (tot, obs_own, e_own, e_edge, d_own, x_edge, wt),
            0,
            [half],
            2 * mm,
        )
        return tot, core, part

    h1_oe, h1_core, part = reduce_obs("a", hx_core, hx_own, avb)
    outs = call(
        bind(second_kernel, norm),
        [chunk] * 4 + [flat, sds((obs + 8, pdev), F32)],
        (scal, part, h1_core, cm, e_core, x_core, bands, w, wt, s0),
        1,
        [full, half, umat, pltpu.VMEM((lev, pdev), F32)],
        5 * mm,
    )
    aparts = shuffle(outs[:4])
    (misfit,) = call(misfit_kernel, [sds((40, pdev), F32)], (h1_oe, h1_core, obs_own, x_core), 0)
    hs, hd_core, part = reduce_obs("b", outs[5], None, outs[4])
    sums = call(sums_kernel, [sds((8, pdev), F32)], (hs, hd_core, misfit, obs_own, x_core), 0)[0]
    bparts = call(
        bind(third_kernel, norm),
        [chunk] * 4,
        (scal, part, hd_core, e_core, x_core, bands, wt),
        1,
        [full, half, umat],
        3 * mm,
    )
    bparts = shuffle(bparts)
    sums = sum4(sums, "tile", tile_xor, (2, 4, 6))
    sums = sums + lax.ppermute(sums, both, far)
    sums = sum4(sums, "tile", tile_xor, (16, 32, 48))
    whole = sds((members, ldev, pdev), F32)
    (grad_first,) = call(grad_first_kernel, [whole], (scal, control, *aparts), 1)
    count = float(members * lev * pdev * tiles)
    grad_second, costs = call(
        bind(grad_second_kernel, count),
        [whole, sds((2,), F32)],
        (scal, control, *aparts, *bparts, sums),
        1,
        out_specs=(VM, SM),
    )
    return grad_first, grad_second, costs


def solution(mesh):
    placed = (
        P(None, "lev", "tile"),
        P(None, "lev", "tile"),
        P("tile", None, None, None),
        P("tile", None),
        P(),
        P(None, "lev"),
        P(None, "tile"),
        P(None, "tile"),
    )
    return jax.shard_map(
        per_device,
        mesh=mesh,
        in_specs=placed,
        out_specs=(P(None, "lev", "tile"), P(None, "lev", "tile"), P()),
        check_vma=False,
    )
```
